32 devices in a mesh: row: 8 (over z, x), col: 4 (over y, core).
Axes of the slice: x: 2, y: 2, z: 4, core: 2. Of those that a mesh axis runs over, the one named last changes fastest.
Arguments:
- x_vectors: bfloat16 [64, 32768], P(None, ('row', 'col')), may hold values from -6 to 6
- w_vectors: bfloat16 [64, 32768], P(None, ('row', 'col')), may hold values from -6 to 6
- order: int32 [32768], P(('row', 'col')), may hold values from 0 to 32767, as said below
- ubasis: bfloat16 [64, 32768], P(None, ('row', 'col')), may hold values from -0.75 to 0.75
- vbasis: bfloat16 [64, 32768], P(None, ('row', 'col')), may hold values from -0.75 to 0.75
- leaf_up_u: bfloat16 [64, 32768], P(None, ('row', 'col')), may hold values from -0.1875 to 0.1875
- leaf_up_v: bfloat16 [64, 32768], P(None, ('row', 'col')), may hold values from -0.1875 to 0.1875
- coupling: bfloat16 [64, 1048576], P(None, ('row', 'col')), may hold values from -0.1875 to 0.1875
- coupling_pairs: int32 [2, 16384], P(None, ('row', 'col')), may hold values from 0 to 511, as said below
- coupling_count: int32 [32], P(('row', 'col')), may hold values from 128 to 512, as said below
- near_blocks: bfloat16 [64, 524288], P(None, ('row', 'col')), may hold values from -0.1875 to 0.1875
- near_pairs: int32 [2, 8192], P(None, ('row', 'col')), may hold values from 0 to 511, as said below
- transfer_u: bfloat16 [64, 3840], replicated, may hold values from -0.5 to 0.5
- transfer_v: bfloat16 [64, 3840], replicated, may hold values from -0.5 to 0.5
- upper_coupling: bfloat16 [64, 3968], replicated, may hold values from -6 to 6
Outputs:
- y_product: bfloat16 [64, 32768], P(None, ('row', 'col'))
- z_product: bfloat16 [64, 32768], P(None, ('row', 'col'))
The draws below stay inside these ranges and needn't reach their ends.
Inputs may be any that keep to these rules, and one draw needn't show every extreme that they name: `order`: each block of 1024 consecutive entries is a permutation of that block's own positions. `coupling_pairs`: for slot b let d = b // 512, r = d // 4, c = d % 4. Entry [0, b] is a leaf of row group r, that is from r * 4 * 16 to (r + 1) * 4 * 16 - 1; entry [1, b] is a leaf l with (l // 16) % 4 == c. Slots of block d from coupling_count[d] onward are not used. `near_pairs`: for slot n let d = n // 256, r = d // 4, c = d % 4. Entry [0, n] is a leaf of row group r as for coupling_pairs; entry [1, n] is a leaf l with t = l // 16, t % 4 == c and t // 4 equal to r - 1, r or r + 1 modulo 8.
All inputs are finite; a program needn't handle non-finite values.
Results may differ from the reference program's by a relative error of at most 0.0063.
Values may be sent and summed in bfloat16 or wider, within the bound.
A program may use at most 192 MiB of HBM per device.

```python
import jax
import jax.numpy as jnp
from jax import lax

LEAF = 64
RANK = 64
NRHS = 64
LPD = 16
COUP_PER = 32
NEAR_PER = 16
ROW_DEVS = 8
COL_DEVS = 4
LEVELS = 5
PIECE = 1024
NLEAF = 512
N = 32768
CPD = 512
NPD = 256
NBLK = 16384
NNEAR = 8192
TNODES = 60
CNODES = 62


def shuffle_one(sub_key):
    return jax.random.permutation(sub_key, PIECE)


def draw_order(key, part):
    dev_count = ROW_DEVS * COL_DEVS
    keys = jax.random.split(key, dev_count)
    shuffled = jax.vmap(shuffle_one)(keys).astype(jnp.int32)
    offsets = jnp.arange(dev_count, dtype=jnp.int32)[:, None] * PIECE
    return (shuffled + offsets).reshape(-1).astype(jnp.int32)


def leaf_pairs(key, per_dev, near_only):
    dev_count = ROW_DEVS * COL_DEVS
    total = per_dev * dev_count
    first_key, second_key, third_key = jax.random.split(key, 3)
    owner = jnp.arange(total, dtype=jnp.int32) // per_dev
    row_group = owner // COL_DEVS
    col_group = owner % COL_DEVS
    row_leaf = row_group * COL_DEVS * LPD + jax.random.randint(first_key, (total,), 0, COL_DEVS * LPD, dtype=jnp.int32)
    if near_only:
        other_row = (row_group + jax.random.randint(second_key, (total,), -1, 2, dtype=jnp.int32)) % ROW_DEVS
    else:
        other_row = jax.random.randint(second_key, (total,), 0, ROW_DEVS, dtype=jnp.int32)
    inner = jax.random.randint(third_key, (total,), 0, LPD, dtype=jnp.int32)
    col_leaf = (other_row * COL_DEVS + col_group) * LPD + inner
    return jnp.stack([row_leaf, col_leaf]).astype(jnp.int32)


def draw_coupling_pairs(key, part):
    return leaf_pairs(jax.random.fold_in(key, 11), CPD, False)


def draw_near_pairs(key, part):
    return leaf_pairs(jax.random.fold_in(key, 23), NPD, True)


def draw_coupling_count(key, part):
    dev_count = ROW_DEVS * COL_DEVS
    first_key, second_key = jax.random.split(jax.random.fold_in(key, 37))
    shifts = jax.random.randint(first_key, (dev_count,), 0, 3, dtype=jnp.int32)
    forced = jax.random.randint(second_key, (), 0, dev_count, dtype=jnp.int32)
    shifts = jnp.where(jnp.arange(dev_count, dtype=jnp.int32) == forced, 0, shifts)
    return jnp.right_shift(jnp.full((dev_count,), CPD, jnp.int32), shifts).astype(jnp.int32)


def level_of(rng, extent, shards, least, high):
    gain = 1.0
    for position, shards_of in shards:
        draws = jax.random.uniform(jax.random.fold_in(jax.random.fold_in(rng, 6), position), (shards_of,), jnp.float32, least / len(shards), high / len(shards))
        gain = gain * jnp.repeat(jnp.exp(draws), extent[position] // shards_of).reshape((-1,) + (1,) * (len(extent) - 1 - position))
    return gain


def bell_draw(key, shape, deviation, most, cuts=(), kind=jnp.bfloat16):
    result = jax.random.normal(key, shape, jnp.float32) * deviation
    if len(cuts) > 0:
        result = level_of(key, shape, cuts, -0.22, 0.18) * result
    return jnp.clip(result, min=-most, max=most).astype(kind)


def setup_inputs(seed: int = 0) -> dict:
    key_list = jax.random.split(jax.random.key(seed), 16)
    x_vectors = bell_draw(key_list[0], (NRHS, N), 1.0, 6.0, ((1, 32),))
    w_vectors = bell_draw(key_list[1], (NRHS, N), 1.0, 6.0, ((1, 32),))
    order = draw_order(jax.random.fold_in(key_list[15], 71), 0)
    ubasis = bell_draw(key_list[3], (RANK, N), LEAF ** -0.5, 0.75, ((1, 32),))
    vbasis = bell_draw(key_list[4], (RANK, N), LEAF ** -0.5, 0.75, ((1, 32),))
    leaf_up_u = bell_draw(key_list[5], (RANK, NLEAF * RANK), (RANK * LPD) ** -0.5, 0.1875, ((1, 32),))
    leaf_up_v = bell_draw(key_list[6], (RANK, NLEAF * RANK), (RANK * LPD) ** -0.5, 0.1875, ((1, 32),))
    coupling = bell_draw(key_list[7], (RANK, NBLK * RANK), (RANK * COUP_PER // 2) ** -0.5, 0.1875, ((1, 32),))
    coupling_pairs = draw_coupling_pairs(jax.random.fold_in(key_list[15], 71), 0)
    coupling_count = draw_coupling_count(jax.random.fold_in(key_list[15], 71), 0)
    near_blocks = bell_draw(key_list[10], (LEAF, NNEAR * LEAF), (LEAF * NEAR_PER) ** -0.5, 0.1875, ((1, 32),))
    near_pairs = draw_near_pairs(jax.random.fold_in(key_list[15], 71), 0)
    transfer_u = bell_draw(key_list[12], (RANK, TNODES * RANK), (2 * RANK) ** -0.5, 0.5)
    transfer_v = bell_draw(key_list[13], (RANK, TNODES * RANK), (2 * RANK) ** -0.5, 0.5)
    upper_coupling = bell_draw(key_list[14], (RANK, CNODES * RANK), (LPD ** 0.5 * RANK ** -0.5), 6.0)
    return dict(x_vectors=x_vectors, w_vectors=w_vectors, order=order, ubasis=ubasis, vbasis=vbasis, leaf_up_u=leaf_up_u, leaf_up_v=leaf_up_v, coupling=coupling, coupling_pairs=coupling_pairs, coupling_count=coupling_count, near_blocks=near_blocks, near_pairs=near_pairs, transfer_u=transfer_u, transfer_v=transfer_v, upper_coupling=upper_coupling)


HIGHEST_PRECISION = lax.Precision.HIGHEST


def rounded(value):
    return lax.optimization_barrier(value.astype(jnp.bfloat16)).astype(jnp.float32)


def level_blocks(matrix_set, dev_count, level):
    node_count = dev_count >> level
    offset = 2 * dev_count - 2 * node_count
    columns = matrix_set[:, offset * RANK:(offset + node_count) * RANK]
    return columns.reshape(RANK, node_count, RANK).astype(jnp.float32)


def reference(x_vectors, w_vectors, order, ubasis, vbasis, leaf_up_u, leaf_up_v, coupling, coupling_pairs, coupling_count, near_blocks, near_pairs, transfer_u, transfer_v, upper_coupling):
    dev_count = ROW_DEVS * COL_DEVS
    leaf_total = dev_count * LPD
    x_perm = jnp.take(x_vectors, order, axis=1)
    w_perm = jnp.take(w_vectors, order, axis=1)
    x_leaves = x_perm.reshape(NRHS, leaf_total, LEAF).astype(jnp.float32)
    w_leaves = w_perm.reshape(NRHS, leaf_total, LEAF).astype(jnp.float32)
    v_leaves = vbasis.reshape(RANK, leaf_total, LEAF).astype(jnp.float32)
    u_leaves = ubasis.reshape(RANK, leaf_total, LEAF).astype(jnp.float32)
    x_coef = rounded(jnp.einsum("qlk,rlk->qlr", x_leaves, v_leaves))
    w_coef = rounded(jnp.einsum("qlk,rlk->qlr", w_leaves, u_leaves))
    up_v = leaf_up_v.reshape(RANK, dev_count, LPD, RANK).astype(jnp.float32)
    up_u = leaf_up_u.reshape(RANK, dev_count, LPD, RANK).astype(jnp.float32)
    x_node = rounded(jnp.einsum("qplr,rpls->pqs", x_coef.reshape(NRHS, dev_count, LPD, RANK), up_v))
    w_node = rounded(jnp.einsum("qplr,rpls->pqs", w_coef.reshape(NRHS, dev_count, LPD, RANK), up_u))

    y_terms = []
    z_terms = []
    for level in range(LEVELS):
        node_count = dev_count >> level
        sibling = jnp.arange(node_count, dtype=jnp.int32) ^ 1
        couple = level_blocks(upper_coupling, dev_count, level)
        y_terms.append(jnp.einsum("aqt,sat->aqs", x_node[sibling], couple))
        z_terms.append(jnp.einsum("aqs,sat->aqt", w_node[sibling], couple[:, sibling]))
        if level < LEVELS - 1:
            moved_x = jnp.einsum("aqr,ras->aqs", x_node, level_blocks(transfer_v, dev_count, level))
            moved_w = jnp.einsum("aqr,ras->aqs", w_node, level_blocks(transfer_u, dev_count, level))
            x_node = rounded(moved_x[0::2] + moved_x[1::2])
            w_node = rounded(moved_w[0::2] + moved_w[1::2])

    y_down = y_terms[LEVELS - 1]
    z_down = z_terms[LEVELS - 1]
    for level in range(LEVELS - 2, -1, -1):
        from_u = level_blocks(transfer_u, dev_count, level)
        from_v = level_blocks(transfer_v, dev_count, level)
        y_down = y_terms[level] + jnp.einsum("aqs,ras->aqr", jnp.repeat(y_down, 2, axis=0), from_u, precision=HIGHEST_PRECISION)
        z_down = z_terms[level] + jnp.einsum("aqs,ras->aqr", jnp.repeat(z_down, 2, axis=0), from_v, precision=HIGHEST_PRECISION)
    y_leafdown = jnp.einsum("pqs,rpls->qplr", y_down, up_u, precision=HIGHEST_PRECISION).reshape(NRHS, leaf_total, RANK)
    z_leafdown = jnp.einsum("pqs,rpls->qplr", z_down, up_v, precision=HIGHEST_PRECISION).reshape(NRHS, leaf_total, RANK)

    def add_couplings(device, sums):
        y_sum, z_sum = sums
        begin = (device * CPD).astype(jnp.int32)
        blocks = lax.dynamic_slice_in_dim(coupling, begin * RANK, CPD * RANK, 1)
        blocks = blocks.reshape(RANK, CPD, RANK).astype(jnp.float32)
        slot_pairs = lax.dynamic_slice_in_dim(coupling_pairs, begin, CPD, 1)
        live_mask = (jnp.arange(CPD, dtype=jnp.int32) < coupling_count[device]).astype(jnp.float32)[None, :, None]
        x_sel = jnp.take(x_coef, slot_pairs[1], axis=1)
        w_sel = jnp.take(w_coef, slot_pairs[0], axis=1)
        y_part = jnp.einsum("qbt,sbt->qbs", x_sel, blocks) * live_mask
        z_part = jnp.einsum("qbs,sbt->qbt", w_sel, blocks) * live_mask
        return y_sum.at[:, slot_pairs[0]].add(y_part), z_sum.at[:, slot_pairs[1]].add(z_part)

    zeros_coef = jnp.zeros((NRHS, leaf_total, RANK), jnp.float32)
    y_sum, z_sum = lax.fori_loop(0, dev_count, add_couplings, (zeros_coef, zeros_coef))

    def add_near(device, sums):
        y_raw, z_raw = sums
        begin = (device * NPD).astype(jnp.int32)
        blocks = lax.dynamic_slice_in_dim(near_blocks, begin * LEAF, NPD * LEAF, 1)
        blocks = blocks.reshape(LEAF, NPD, LEAF).astype(jnp.float32)
        slot_pairs = lax.dynamic_slice_in_dim(near_pairs, begin, NPD, 1)
        x_sel = jnp.take(x_leaves, slot_pairs[1], axis=1)
        w_sel = jnp.take(w_leaves, slot_pairs[0], axis=1)
        y_part = jnp.einsum("qnb,anb->qna", x_sel, blocks)
        z_part = jnp.einsum("qna,anb->qnb", w_sel, blocks)
        return y_raw.at[:, slot_pairs[0]].add(y_part), z_raw.at[:, slot_pairs[1]].add(z_part)

    zeros_raw = jnp.zeros((NRHS, leaf_total, LEAF), jnp.float32)
    y_raw, z_raw = lax.fori_loop(0, dev_count, add_near, (zeros_raw, zeros_raw))

    y_leaf = rounded(y_sum + y_leafdown)
    z_leaf = rounded(z_sum + z_leafdown)
    y_points = jnp.einsum("qlr,rlk->qlk", y_leaf, u_leaves) + y_raw
    z_points = jnp.einsum("qlr,rlk->qlk", z_leaf, v_leaves) + z_raw
    y_perm = y_points.reshape(NRHS, N).astype(jnp.bfloat16)
    z_perm = z_points.reshape(NRHS, N).astype(jnp.bfloat16)
    y_out = jnp.zeros((NRHS, N), jnp.bfloat16).at[:, order].set(y_perm)
    z_out = jnp.zeros((NRHS, N), jnp.bfloat16).at[:, order].set(z_perm)
    return (y_out, z_out)
```

```python
import functools

import jax
import jax.numpy as jnp
from jax import lax
from jax.experimental import pallas as pl
from jax.experimental.pallas import tpu as pltpu
from jax.sharding import PartitionSpec as P

BF = jnp.bfloat16
F32 = jnp.float32
VMEM = pl.BlockSpec(memory_space=pltpu.VMEM)
SMEM = pl.BlockSpec(memory_space=pltpu.SMEM)
NN = (((1,), (0,)), ((), ()))
NT = (((1,), (1,)), ((), ()))
UNROLL = 4


def mm(a, b, dims=NN):
    return lax.dot_general(a, b, dims, preferred_element_type=F32)


def left_mask(half, dtype):
    lane = lax.broadcasted_iota(jnp.int32, (1, 2 * half), 1)
    return (lane < half).astype(F32).astype(dtype), (lane >= half).astype(F32).astype(dtype)


def diag2(v, ml, mr):
    return jnp.concatenate([v * ml, v * mr], axis=0)


def quot(v, n):
    return lax.shift_right_logical(v, n.bit_length() - 1) if n & (n - 1) == 0 else lax.div(v, n)


def mod(v, n):
    return lax.bitwise_and(v, n - 1) if n & (n - 1) == 0 else lax.rem(v, n)


def split2(v):
    hi = v.astype(BF)
    return hi, (v - hi.astype(F32)).astype(BF)


def mm2(v, b, dims):
    hi, lo = split2(v)
    return mm(hi, b, dims) + mm(lo, b, dims)


def one_hot(order_ref, base):
    n = order_ref.shape[1]
    src = lax.broadcasted_iota(jnp.int32, (n, n), 0)
    return jnp.where(src == order_ref[...] - base, 1.0, 0.0).astype(BF)


def twin_eye(half):
    row = lax.broadcasted_iota(jnp.int32, (half, 2 * half), 0)
    lane = lax.broadcasted_iota(jnp.int32, (half, 2 * half), 1)
    return jnp.where(jnp.logical_or(lane == row, lane == row + half), 1.0, 0.0).astype(BF)


def grid_of(rows):
    inner = 1 << ((rows.bit_length() - 1) // 2)
    return rows // inner, inner


def greet(rows, cols, r, c):
    bar = pltpu.get_barrier_semaphore()
    for d in range(1, rows):
        pl.semaphore_signal(bar, inc=1, device_id={"row": lax.rem(r + d, rows)}, device_id_type=pl.DeviceIdType.MESH)
    for d in range(1, cols):
        pl.semaphore_signal(bar, inc=1, device_id={"col": lax.rem(c + d, cols)}, device_id_type=pl.DeviceIdType.MESH)
    return bar


def push(src, dst, sems, at, axis, peer):
    copy = pltpu.make_async_remote_copy(
        src_ref=src,
        dst_ref=dst,
        send_sem=sems.at[(0, *at)],
        recv_sem=sems.at[(1, *at)],
        device_id={axis: peer},
        device_id_type=pl.DeviceIdType.MESH,
    )
    copy.start()
    return copy


def chunk_at(ref, at, wide):
    return ref[:, pl.ds(pl.multiple_of(at * wide, wide), wide)]


def combine(v0, v1, fv, fu, ml, mr, isl, half):
    xp = jnp.where(isl, v0, pltpu.roll(v1, half, 1)).astype(BF)
    wp = jnp.where(isl, pltpu.roll(v0, half, 1), v1).astype(BF)
    x = mm(xp, diag2(fv, ml, mr))
    w = mm(wp, diag2(fu, ml, mr))
    return jnp.where(isl, x + pltpu.roll(x, half, 1), w + pltpu.roll(w, half, 1)).astype(BF)


def first_kernel(token_ref):
    token_ref[...] = jnp.zeros(token_ref.shape, token_ref.dtype)


def up_kernel(rows, cols, token_ref, x_ref, w_ref, order_ref, v_ref, u_ref, ev_ref, eu_ref, fu_ref, fv_ref,
              xc_ref, xp_ref, wa_ref, n0_ref, n2_ref, na_sem, nb_sem, z_sem, x_sem, p_sem, w_sem):
    q, n = x_ref.shape
    packs = xc_ref.shape[1]
    wide = xc_ref.shape[3]
    half = wide // 2
    deep, inner = grid_of(rows)
    r = lax.axis_index("row")
    c = lax.axis_index("col")
    zi = r // inner
    xi = lax.rem(r, inner)
    bar = greet(rows, cols, r, c)
    ml, mr = left_mask(half, BF)
    isl = lax.broadcasted_iota(jnp.int32, (q, wide), 1) < half
    eye = twin_eye(half)
    hot = one_hot(order_ref, (r * cols + c) * n)
    both = mm(jnp.concatenate([x_ref[...], w_ref[...]], axis=0), hot).astype(BF)
    folds = []
    for side, (b_ref, e_ref) in enumerate(((v_ref, ev_ref), (u_ref, eu_ref))):
        pts = both[side * q:(side + 1) * q]
        node = jnp.zeros((q, wide), F32)
        for m in range(packs):
            cs = slice(m * wide, (m + 1) * wide)
            pm = pts[:, cs]
            cm = mm(pm, diag2(b_ref[:, cs], ml, mr), NT).astype(BF)
            if side == 0:
                turned = diag2(pm, ml, mr)
                xc_ref[r, m] = mm(b_ref[:, cs], turned, NT).astype(BF)
                xp_ref[1, m] = mm(eye, turned, NT).astype(BF)
            else:
                wa_ref[c, 0, m] = cm
                wa_ref[c, 1, m] = pm
            node = node + mm(cm, diag2(e_ref[:, cs], ml, mr))
        folds.append(node + pltpu.roll(node, half, 1))
    n0_ref[c] = jnp.where(isl, folds[0], folds[1]).astype(BF)
    pl.semaphore_wait(bar, rows + cols - 2)
    node_a = [
        push(n0_ref.at[c], n0_ref.at[c], na_sem, (d - 1,), "col", lax.rem(c + d, cols)) for d in range(1, cols)
    ]
    own = xc_ref.at[r]
    along = [
        push(own, own, z_sem, (d - 1,), "row", lax.rem(zi + d, deep) * inner + xi) for d in range(1, deep)
    ]
    across = [
        push(own, own, x_sem, (0, d - 1), "row", zi * inner + lax.rem(xi + d, inner)) for d in range(1, inner)
    ]
    points = [
        push(xp_ref.at[1], xp_ref.at[0], p_sem, (0,), "row", lax.rem(r + 1, rows)),
        push(xp_ref.at[1], xp_ref.at[2], p_sem, (1,), "row", lax.rem(r + rows - 1, rows)),
    ]
    wide_w = [
        push(wa_ref.at[c], wa_ref.at[c], w_sem, (d - 1,), "col", lax.rem(c + d, cols)) for d in range(1, cols)
    ]
    for copy in node_a:
        copy.wait_recv()
    dev_count = rows * cols
    vals = [n0_ref[i].astype(F32) for i in range(cols)]
    level = 0
    while len(vals) > 1:
        off = dev_count - (dev_count >> level)
        count = len(vals) // 2
        nxt = []
        for i in range(count):
            at = off + r * count + i
            nxt.append(
                combine(vals[2 * i], vals[2 * i + 1], chunk_at(fv_ref, at, wide), chunk_at(fu_ref, at, wide), ml, mr, isl, half)
            )
        vals = [v.astype(F32) for v in nxt]
        level += 1
    n2_ref[r] = vals[0].astype(BF)
    node_b = [
        push(n2_ref.at[r], n2_ref.at[r], nb_sem, (d - 1,), "row", lax.rem(r + d, rows)) for d in range(1, rows)
    ]
    for d in range(1, deep):
        along[d - 1].wait_recv()
        got = xc_ref.at[lax.rem(zi + deep - d, deep) * inner + xi]
        across += [
            push(got, got, x_sem, (d, e - 1), "row", zi * inner + lax.rem(xi + e, inner)) for e in range(1, inner)
        ]
    for copy in node_b + across + points + wide_w:
        copy.wait_recv()
    for copy in node_a + node_b + along + across + points + wide_w:
        copy.wait_send()


def slot_kernel(unroll, cp_ref, np_ref, live_ref, x_ref, p_ref, w_ref, s_ref, d_ref, y_ref, z_ref, n_ref,
                xl, xr, ql, qr, wc, wp, yc, yn, zc, zn, y0, y1, z0, z1):
    rows, packs, q, wide = x_ref.shape
    cols = w_ref.shape[0]
    half = wide // 2
    leaves = 2 * packs
    live = live_ref[0]
    my_row = lax.axis_index("row")
    row_base = my_row * cols * leaves
    isl = lax.broadcasted_iota(jnp.int32, (q, wide), 1) < half
    lane = lax.broadcasted_iota(jnp.int32, (q, wide), 1)
    none = jnp.zeros((q, wide), BF)
    blank = jnp.zeros((q, wide), F32)

    def clear(acc):
        group = 8
        def step(i, carry):
            for k in range(group):
                acc[i * group + k] = blank
            return carry
        lax.fori_loop(0, acc.shape[0] // group, step, 0)

    for acc in (yc, yn, zc, zn):
        clear(acc)

    def split(src, left, right, at):
        v = src[...]
        r = jnp.concatenate([v[:, half:], v[:, :half]], axis=1)
        left[at] = jnp.where(isl, v, none)
        left[at + 1] = jnp.where(isl, r, none)
        right[at] = jnp.where(isl, none, r)
        right[at + 1] = jnp.where(isl, none, v)

    def widen(src, table, at):
        v = src[...]
        r = jnp.concatenate([v[:, half:], v[:, :half]], axis=1)
        table[at] = jnp.where(isl, v, r)
        table[at + 1] = jnp.where(isl, r, v)

    def fill_x(i, carry):
        for m in range(packs):
            split(x_ref.at[i, m], xl, xr, 2 * (i * packs + m))
        return carry

    def fill_w(i, carry):
        for m in range(packs):
            widen(w_ref.at[i, 0, m], wc, 2 * (i * packs + m))
            widen(w_ref.at[i, 1, m], wp, 2 * (i * packs + m))
        return carry

    def fill_p(i, carry):
        for m in range(packs):
            split(p_ref.at[i, m], ql, qr, 2 * (i * packs + m))
        return carry

    lax.fori_loop(0, rows, fill_x, 0)
    lax.fori_loop(0, cols, fill_w, 0)
    lax.fori_loop(0, 3, fill_p, 0)

    def place(pairs, b, near):
        leaf = pairs[1, b]
        group = quot(leaf, cols * leaves)
        if near:
            group = mod(group - my_row + (rows + 1), rows)
        return pairs[0, b] - row_base, group * leaves + mod(leaf, leaves)

    def run(pairs, mat, lt, rt, wt, ya, za, near, steps):
        def settle(g, yb, zb):
            for k in range(unroll):
                p = g * unroll + k
                i0, j0 = place(pairs, 2 * p, near)
                i1, j1 = place(pairs, 2 * p + 1, near)
                yv = yb[k]
                zv = zb[k]
                a = ya[i0, :, :half] + yv[:, :half]
                b = ya[i1, :, half:] + yv[:, half:]
                c = za[j0, :, :half] + zv[:, :half]
                d = za[j1, :, half:] + zv[:, half:]
                ya[i0, :, :half] = a
                ya[i1, :, half:] = b
                za[j0, :, :half] = c
                za[j1, :, half:] = d

        def multiply(g, yb, zb):
            for k in range(unroll):
                p = g * unroll + k
                i0, j0 = place(pairs, 2 * p, near)
                i1, j1 = place(pairs, 2 * p + 1, near)
                blk = mat[:, pl.ds(pl.multiple_of(p * wide, wide), wide)]
                if not near:
                    reach = jnp.where(2 * p + 1 < live, wide, jnp.where(2 * p < live, half, 0))
                    blk = jnp.where(lane < reach, blk, none)
                pair = jnp.concatenate([jnp.where(isl, blk, none), jnp.where(isl, none, blk)], axis=0)
                xs = jnp.concatenate([lt[j0], rt[j1]], axis=0)
                ws = jnp.where(isl, wt[i0], wt[i1])
                yb[k] = mm(blk, xs)
                zb[k] = mm(ws, pair)

        multiply(0, y0, z0)
        def step(g, carry):
            multiply(2 * g + 1, y1, z1)
            settle(2 * g, y0, z0)
            multiply(2 * g + 2, y0, z0)
            settle(2 * g + 1, y1, z1)
            return carry
        lax.fori_loop(0, steps - 1, step, 0)
        multiply(2 * steps - 1, y1, z1)
        settle(2 * steps - 2, y0, z0)
        settle(2 * steps - 1, y1, z1)

    run(np_ref, d_ref, ql, qr, wp, yn, zn, True, np_ref.shape[1] // (4 * unroll))
    run(cp_ref, s_ref, xl, xr, wc, yc, zc, False, quot(live + 4 * unroll - 1, 4 * unroll))

    def fold(acc, at):
        a, b = acc[at], acc[at + 1]
        return jnp.where(isl, a, b) + pltpu.roll(jnp.where(isl, b, a), half, 1)

    def out_y(i, carry):
        for m in range(packs):
            y_ref[i, 0, m] = fold(yc, 2 * (i * packs + m)).astype(y_ref.dtype)
            y_ref[i, 1, m] = fold(yn, 2 * (i * packs + m)).astype(y_ref.dtype)
        return carry

    def out_z(i, carry):
        for m in range(packs):
            z_ref[i, m] = fold(zc, 2 * (i * packs + m)).astype(z_ref.dtype)
        return carry

    def out_n(i, carry):
        for m in range(packs):
            n_ref[i, m] = fold(zn, 2 * (i * packs + m)).astype(n_ref.dtype)
        return carry

    lax.fori_loop(0, cols, out_y, 0)
    lax.fori_loop(0, rows, out_z, 0)
    lax.fori_loop(0, 3, out_n, 0)


def down_kernel(rows, cols, y_ref, z_ref, n_ref, n0_ref, n2_ref, order_ref, u_ref, v_ref, eu_ref, ev_ref, fu_ref, fv_ref,
                s_ref, o_ref, y_in, z1_in, z1_out, z2_in, zn_in, nodes, y_sem, z1_sem, z2_sem, n_sem):
    _, packs, q, wide = z_ref.shape
    half = wide // 2
    deep, inner = grid_of(rows)
    dev_count = rows * cols
    r = lax.axis_index("row")
    c = lax.axis_index("col")
    me = r * cols + c
    zi = r // inner
    xi = lax.rem(r, inner)
    bar = greet(rows, cols, r, c)
    ml, mr = left_mask(half, BF)
    isl = lax.broadcasted_iota(jnp.int32, (q, wide), 1) < half
    hot = one_hot(order_ref, me * order_ref.shape[1])
    eye = twin_eye(half)
    pl.semaphore_wait(bar, rows + cols - 2)
    first = {}
    for d in list(range(1, deep)) + [0]:
        to = lax.rem(zi + d, deep) * inner
        first[d] = []
        for e in range(1, inner):
            peer = lax.rem(xi + e, inner)
            first[d].append(
                push(z_ref.at[to + peer], z1_in.at[d, e - 1], z1_sem, (d, e - 1), "row", zi * inner + peer)
            )
    near = [
        push(n_ref.at[0], zn_in.at[0], n_sem, (0,), "row", lax.rem(r + rows - 1, rows)),
        push(n_ref.at[2], zn_in.at[1], n_sem, (1,), "row", lax.rem(r + 1, rows)),
    ]
    y_copies = []
    for d in range(1, cols):
        peer = lax.rem(c + d, cols)
        y_copies.append(push(y_ref.at[peer], y_in.at[d - 1], y_sem, (d - 1,), "col", peer))

    second = []
    for d in range(1, deep):
        for copy in first[d]:
            copy.wait_recv()
        to = lax.rem(zi + d, deep) * inner + xi
        for m in range(packs):
            total = z_ref[to, m].astype(F32)
            for e in range(inner - 1):
                total = total + z1_in[d, e, m].astype(F32)
            z1_out[d - 1, m] = total.astype(BF)
        second.append(push(z1_out.at[d - 1], z2_in.at[d - 1], z2_sem, (d - 1,), "row", to))

    levels = dev_count.bit_length() - 1
    starts = []
    at = 0
    vals = None
    for level in range(levels):
        if level == 0:
            vals = [n0_ref[i].astype(F32) for i in range(cols)]
            split = r
        elif cols >> level == 1:
            vals = [n2_ref[i].astype(F32) for i in range(rows)]
            split = 0
        starts.append((at, c >> level if cols >> level > 1 else me >> level))
        for i, v in enumerate(vals):
            nodes[at + i] = v
        at += len(vals)
        off = dev_count - (dev_count >> level)
        count = len(vals) // 2
        if level < levels - 1 and count * 2 == len(vals) and not (cols >> level == 2):
            vals = [
                combine(
                    vals[2 * i],
                    vals[2 * i + 1],
                    chunk_at(fv_ref, off + split * count + i, wide),
                    chunk_at(fu_ref, off + split * count + i, wide),
                    ml, mr, isl, half,
                ).astype(F32)
                for i in range(count)
            ]

    lane_half = (lax.broadcasted_iota(jnp.int32, (q, wide), 1) >= half).astype(jnp.int32)

    def turned(v, chunk, side):
        return mm2(jnp.where(lane_half == side, v, 0.0), jnp.concatenate([chunk, chunk], axis=0), NT)

    y_down = z_down = None
    for level in range(levels - 1, -1, -1):
        start, local = starts[level]
        own = me >> level
        side = lax.rem(own, 2)
        sib = nodes[start + local + 1 - 2 * lax.rem(local, 2)]
        rolled = pltpu.roll(sib, half, 1)
        xs = jnp.where(isl, sib, rolled)
        ws = jnp.where(isl, rolled, 0.0).astype(BF)
        at = dev_count - (dev_count >> level) + own // 2
        cup = chunk_at(s_ref, at, wide)
        dup = jnp.concatenate([cup, cup], axis=0)
        y_term = mm(jnp.where(lane_half == side, xs, 0.0).astype(BF), dup, NT)
        z_raw = jnp.where(lane_half == 1 - side, mm(ws, dup), 0.0)
        z_term = z_raw + pltpu.roll(z_raw, half, 1)
        if level < levels - 1:
            y_term = y_term + turned(y_down, chunk_at(fu_ref, at, wide), side)
            z_term = z_term + turned(z_down, chunk_at(fv_ref, at, wide), side)
        y_down, z_down = y_term, z_term

    perms = []
    for flip, (down, b_ref, e_ref) in enumerate(((y_down, u_ref, eu_ref), (z_down, v_ref, ev_ref))):
        if flip == 0:
            for copy in y_copies:
                copy.wait_recv()
        else:
            for copy in first[0] + second + near:
                copy.wait_recv()
        parts = []
        for m in range(packs):
            cs = slice(m * wide, (m + 1) * wide)
            if flip == 0:
                coef, raw = y_ref[c, 0, m].astype(F32), y_ref[c, 1, m].astype(F32)
                for d in range(cols - 1):
                    coef = coef + y_in[d, 0, m].astype(F32)
                    raw = raw + y_in[d, 1, m].astype(F32)
            else:
                coef, raw = z_ref[r, m].astype(F32), n_ref[1, m].astype(F32)
                for e in range(inner - 1):
                    coef = coef + z1_in[0, e, m].astype(F32)
                for d in range(deep - 1):
                    coef = coef + z2_in[d, m].astype(F32)
                for k in range(2):
                    raw = raw + zn_in[k, m].astype(F32)
            if flip == 0:
                hi, lo = split2(down)
                e = e_ref[:, cs]
                leaf = (coef + mm(e, diag2(hi, ml, mr), NT) + mm(e, diag2(lo, ml, mr), NT)).astype(BF)
                turned = mm(eye, diag2(b_ref[:, cs], ml, mr), NT).astype(BF)
                pts = (mm(turned, diag2(leaf, ml, mr)) + raw).astype(BF)
                parts.append(mm(eye, diag2(pts, ml, mr), NT).astype(BF))
            else:
                leaf = (coef + mm2(down, diag2(e_ref[:, cs], ml, mr), NT)).astype(BF)
                parts.append((mm(leaf, diag2(b_ref[:, cs], ml, mr)) + raw).astype(BF))
        perms.append(jnp.concatenate(parts, axis=1))
    o_ref[...] = mm(jnp.concatenate(perms, axis=0), hot, NT).astype(BF)
    for copies in (*first.values(), second, near, y_copies):
        for copy in copies:
            copy.wait_send()


def per_device(
    x_vectors,
    w_vectors,
    order,
    ubasis,
    vbasis,
    leaf_up_u,
    leaf_up_v,
    coupling,
    coupling_pairs,
    coupling_count,
    near_blocks,
    near_pairs,
    transfer_u,
    transfer_v,
    upper_coupling,
):
    q, piece = x_vectors.shape
    rank = ubasis.shape[0]
    leaves = leaf_up_u.shape[1] // rank
    packs = leaves // 2
    wide = 2 * rank
    rows = lax.axis_size("row")
    cols = lax.axis_size("col")
    deep, inner = grid_of(rows)
    order2 = order.reshape(1, piece)

    def shape(*lead):
        return jax.ShapeDtypeStruct((*lead, q, wide), BF)

    def buf(*lead, dtype=BF):
        return pltpu.VMEM((*lead, q, wide), dtype)

    def sems(*lead):
        return pltpu.SemaphoreType.DMA((2, *lead))

    def params(mib, cid=None):
        limit = mib * 1024 * 1024
        if cid is None:
            return pltpu.CompilerParams(vmem_limit_bytes=limit)
        return pltpu.CompilerParams(vmem_limit_bytes=limit, collective_id=cid, has_side_effects=True)

    token = pl.pallas_call(
        first_kernel,
        out_shape=jax.ShapeDtypeStruct((1, wide), F32),
        out_specs=VMEM,
        compiler_params=params(1),
        cost_estimate=pl.CostEstimate(flops=2_000_000_000, bytes_accessed=6_000_000, transcendentals=0),
    )()
    loaded = (token, x_vectors, w_vectors, order2, vbasis, ubasis, leaf_up_v, leaf_up_u, transfer_u, transfer_v)
    x_all, x_pts, w_all, n0, n2 = pl.pallas_call(
        functools.partial(up_kernel, rows, cols),
        out_shape=(shape(rows, packs), shape(3, packs), shape(cols, 2, packs), shape(cols), shape(rows)),
        in_specs=[VMEM] * 10,
        out_specs=(VMEM,) * 5,
        scratch_shapes=[
            sems(cols - 1),
            sems(rows - 1),
            sems(deep - 1),
            sems(deep, inner - 1),
            sems(2),
            sems(cols - 1),
        ],
        compiler_params=params(16, 0),
        cost_estimate=pl.CostEstimate(flops=20_000_000_000, bytes_accessed=60_000_000, transcendentals=0),
    )(*loaded)
    unroll = UNROLL
    tables = 2 * leaves * (rows + 3 + cols)
    sums = leaves * (2 * cols + rows + 3) + 4 * unroll
    y_part, z_part, n_part = pl.pallas_call(
        functools.partial(slot_kernel, unroll),
        out_shape=(shape(cols, 2, packs), shape(rows, packs), shape(3, packs)),
        in_specs=[SMEM] * 3 + [VMEM] * 5,
        out_specs=(VMEM,) * 3,
        scratch_shapes=[
            buf(rows * leaves),
            buf(rows * leaves),
            buf(3 * leaves),
            buf(3 * leaves),
            buf(cols * leaves),
            buf(cols * leaves),
            buf(cols * leaves, dtype=F32),
            buf(cols * leaves, dtype=F32),
            buf(rows * leaves, dtype=F32),
            buf(3 * leaves, dtype=F32),
            buf(unroll, dtype=F32),
            buf(unroll, dtype=F32),
            buf(unroll, dtype=F32),
            buf(unroll, dtype=F32),
        ],
        compiler_params=params(8 + (tables * q * wide * 2 + sums * q * wide * 4) // 1024**2),
        cost_estimate=pl.CostEstimate(flops=20_000_000_000, bytes_accessed=60_000_000, transcendentals=0),
    )(coupling_pairs, near_pairs, coupling_count, x_all, x_pts, w_all, coupling, near_blocks)
    out = pl.pallas_call(
        functools.partial(down_kernel, rows, cols),
        out_shape=jax.ShapeDtypeStruct((2 * q, piece), BF),
        in_specs=[VMEM] * 13,
        out_specs=VMEM,
        scratch_shapes=[
            buf(cols - 1, 2, packs),
            buf(deep, inner - 1, packs),
            buf(deep - 1, packs),
            buf(deep - 1, packs),
            buf(2, packs),
            buf(2 * (rows + cols), dtype=F32),
            sems(cols - 1),
            sems(deep, inner - 1),
            sems(deep - 1),
            sems(2),
        ],
        compiler_params=params(16, 1),
    )(
        y_part, z_part, n_part, n0, n2, order2, ubasis, vbasis, leaf_up_u, leaf_up_v,
        transfer_u, transfer_v, upper_coupling,
    )
    return out[:q], out[q:]


def solution(mesh):
    both = P(None, ("row", "col"))
    flat = P(("row", "col"))
    return jax.shard_map(
        per_device,
        mesh=mesh,
        in_specs=(both, both, flat, both, both, both, both, both, both, flat, both, both, P(), P(), P()),
        out_specs=(both, both),
        check_vma=False,
    )
```

```python
import functools

import jax
import jax.numpy as jnp
from jax import lax
from jax.experimental import pallas as pl
from jax.experimental.pallas import tpu as pltpu
from jax.sharding import PartitionSpec as P

BF = jnp.bfloat16
F32 = jnp.float32
VMEM = pl.BlockSpec(memory_space=pltpu.VMEM)
SMEM = pl.BlockSpec(memory_space=pltpu.SMEM)
NN = (((1,), (0,)), ((), ()))
NT = (((1,), (1,)), ((), ()))
UNROLL = 8


def mm(a, b, dims=NN):
    return lax.dot_general(a, b, dims, preferred_element_type=F32)


def left_mask(half, dtype):
    lane = lax.broadcasted_iota(jnp.int32, (1, 2 * half), 1)
    return (lane < half).astype(F32).astype(dtype), (lane >= half).astype(F32).astype(dtype)


def diag2(v, ml, mr):
    return jnp.concatenate([v * ml, v * mr], axis=0)


def quot(v, n):
    return lax.shift_right_logical(v, n.bit_length() - 1) if n & (n - 1) == 0 else lax.div(v, n)


def mod(v, n):
    return lax.bitwise_and(v, n - 1) if n & (n - 1) == 0 else lax.rem(v, n)


def split2(v):
    hi = v.astype(BF)
    return hi, (v - hi.astype(F32)).astype(BF)


def mm2(v, b, dims):
    hi, lo = split2(v)
    return mm(hi, b, dims) + mm(lo, b, dims)


def one_hot(order_ref, base):
    n = order_ref.shape[1]
    src = lax.broadcasted_iota(jnp.int32, (n, n), 0)
    return jnp.where(src == order_ref[...] - base, 1.0, 0.0).astype(BF)


def twin_eye(half):
    row = lax.broadcasted_iota(jnp.int32, (half, 2 * half), 0)
    lane = lax.broadcasted_iota(jnp.int32, (half, 2 * half), 1)
    return jnp.where(jnp.logical_or(lane == row, lane == row + half), 1.0, 0.0).astype(BF)


def grid_of(rows):
    inner = 1 << ((rows.bit_length() - 1) // 2)
    return rows // inner, inner


def greet(rows, cols, r, c):
    bar = pltpu.get_barrier_semaphore()
    for d in range(1, rows):
        pl.semaphore_signal(bar, inc=1, device_id={"row": lax.rem(r + d, rows)}, device_id_type=pl.DeviceIdType.MESH)
    for d in range(1, cols):
        pl.semaphore_signal(bar, inc=1, device_id={"col": lax.rem(c + d, cols)}, device_id_type=pl.DeviceIdType.MESH)
    return bar


def push(src, dst, sems, at, axis, peer):
    copy = pltpu.make_async_remote_copy(
        src_ref=src,
        dst_ref=dst,
        send_sem=sems.at[(0, *at)],
        recv_sem=sems.at[(1, *at)],
        device_id={axis: peer},
        device_id_type=pl.DeviceIdType.MESH,
    )
    copy.start()
    return copy


def chunk_at(ref, at, wide):
    return ref[:, pl.ds(pl.multiple_of(at * wide, wide), wide)]


def combine(v0, v1, fv, fu, ml, mr, isl, half):
    xp = jnp.where(isl, v0, pltpu.roll(v1, half, 1)).astype(BF)
    wp = jnp.where(isl, pltpu.roll(v0, half, 1), v1).astype(BF)
    x = mm(xp, diag2(fv, ml, mr))
    w = mm(wp, diag2(fu, ml, mr))
    return jnp.where(isl, x + pltpu.roll(x, half, 1), w + pltpu.roll(w, half, 1)).astype(BF)


def first_kernel(token_ref):
    token_ref[...] = jnp.zeros(token_ref.shape, token_ref.dtype)


def local_kernel(token_ref, far_ref, near_ref, order_ref, x_ref, w_ref, v_ref, u_ref, ev_ref, eu_ref,
                 xc_ref, xp_ref, w_out, n_ref, fi_ref, fj_ref, ni_ref, nj_ref):
    q, n = x_ref.shape
    packs = xc_ref.shape[0]
    wide = xc_ref.shape[2]
    half = wide // 2
    rows, cols = lax.axis_size("row"), lax.axis_size("col")
    my_row = lax.axis_index("row")
    base = (my_row * cols + lax.axis_index("col")) * n
    leaves = 2 * packs
    for pairs, i_ref, j_ref, near in ((far_ref, fi_ref, fj_ref, False), (near_ref, ni_ref, nj_ref, True)):
        leaf = pairs[1:2]
        group = quot(leaf, cols * leaves)
        if near:
            group = mod(group - my_row + (rows + 1), rows)
        i_ref[...] = pairs[0:1] - my_row * cols * leaves
        j_ref[...] = group * leaves + mod(leaf, leaves)
    ml, mr = left_mask(half, BF)
    isl = lax.broadcasted_iota(jnp.int32, (q, wide), 1) < half
    eye = twin_eye(half)
    hot = one_hot(order_ref, base)
    both = mm(jnp.concatenate([x_ref[...], w_ref[...]], axis=0), hot).astype(BF)
    folds = []
    for side, (b_ref, e_ref) in enumerate(((v_ref, ev_ref), (u_ref, eu_ref))):
        pts = both[side * q:(side + 1) * q]
        node = jnp.zeros((q, wide), F32)
        for m in range(packs):
            cs = slice(m * wide, (m + 1) * wide)
            pm = pts[:, cs]
            cm = mm(pm, diag2(b_ref[:, cs], ml, mr), NT).astype(BF)
            if side == 0:
                turned = diag2(pm, ml, mr)
                xc_ref[m] = mm(b_ref[:, cs], turned, NT).astype(BF)
                xp_ref[m] = mm(eye, turned, NT).astype(BF)
            else:
                w_out[0, m] = cm
                w_out[1, m] = pm
            node = node + mm(cm, diag2(e_ref[:, cs], ml, mr))
        folds.append(node + pltpu.roll(node, half, 1))
    n_ref[...] = jnp.where(isl, folds[0], folds[1]).astype(BF)


class Mail:
    def __init__(self, sem):
        self.sem = sem
        self.sent = []

    def copy(self, src, dst, recv, peer, at):
        return pltpu.make_async_remote_copy(
            src_ref=src,
            dst_ref=dst,
            send_sem=self.sem.at[at],
            recv_sem=recv,
            device_id=peer,
            device_id_type=pl.DeviceIdType.MESH,
        )

    def push(self, src, dst, recv, peer, when=None):
        args = (src, dst, recv, peer, len(self.sent))
        self.sent.append((args, when))
        guarded(when, lambda: self.copy(*args).start())

    def landed(self, dst, recv, peer):
        self.copy(dst, dst, recv, peer, 0).wait_recv()

    def close(self):
        for args, when in self.sent:
            guarded(when, lambda args=args: self.copy(*args).wait_send())


def guarded(when, act):
    if when is None:
        act()
    else:
        pl.when(when)(act)


def place(pairs, p):
    i_ref, j_ref = pairs
    return i_ref[0, 2 * p], i_ref[0, 2 * p + 1], j_ref[0, 2 * p], j_ref[0, 2 * p + 1]


def gather_kernel(rows, cols, unroll, fi_ref, fj_ref, ni_ref, nj_ref, live_ref, xc_own, xp_own, w_own, n_own, fu_ref, fv_ref, s_ref, d_ref,
                  xl, xr, pyn, pzn, pzc, sib_ref,
                  xc, xp, wa, na, nb, ql, qr, wc, wp, send_sem, x_sem, p_sem, w_sem, na_sem, nb_sem):
    packs, q, wide = xc_own.shape
    half = wide // 2
    leaves = 2 * packs
    deep, inner = grid_of(rows)
    outer = cols // 2
    dev_count = rows * cols
    first = (3 * packs) // 8
    cuts = ((0, first), (first, packs - first))
    r = lax.axis_index("row")
    c = lax.axis_index("col")
    zi = r // inner
    xi = lax.rem(r, inner)
    oi = c // 2
    ki = lax.rem(c, 2)
    live = live_ref[0]
    bar = greet(rows, cols, r, c)
    ml, mr = left_mask(half, BF)
    isl = lax.broadcasted_iota(jnp.int32, (q, wide), 1) < half
    lane = lax.broadcasted_iota(jnp.int32, (q, wide), 1)
    none = jnp.zeros((q, wide), BF)
    mail = Mail(send_sem)
    near_row = {"row": lax.rem(r + 1, rows)}
    near_col = {"col": lax.rem(c + 1, cols)}

    def row_of(z, x):
        return {"row": z * inner + x}

    def turn_x(e):
        return lax.rem(xi + e, inner)

    def xpart(row, part):
        return xc.at[row, pl.ds(*cuts[part])]

    def xown(part):
        return xc_own.at[pl.ds(*cuts[part])]

    up, down = zi < deep - 1, zi > 0
    pl.semaphore_wait(bar, rows + cols - 2)

    for e in range(1, cols):
        mail.push(n_own, na.at[c], na_sem.at[c], {"col": lax.rem(c + e, cols)})
    for kind in (1, 0):
        for e in range(1, outer):
            mail.push(w_own.at[kind], wa.at[c, kind], w_sem.at[c, kind], {"col": lax.rem(oi + e, outer) * 2 + ki})
        mail.push(w_own.at[kind], wa.at[c, kind], w_sem.at[c, kind], {"col": oi * 2 + 1 - ki})
    for e in range(1, inner):
        mail.push(xown(0), xpart(r, 0), x_sem.at[r, 0], row_of(zi, turn_x(e)))
    for part in (1, 0):
        mail.push(xown(part), xpart(r, part), x_sem.at[r, part], row_of(zi + 1, xi), up)
        mail.push(xown(part), xpart(r, part), x_sem.at[r, part], row_of(zi - 1, xi), down)
    if inner == 2:
        mail.push(xp_own, xp.at[2 * xi], p_sem.at[2 * xi], row_of(zi, 1 - xi))
    else:
        mail.push(xp_own, xp.at[0], p_sem.at[0], {"row": lax.rem(r + 1, rows)})
        mail.push(xp_own, xp.at[2], p_sem.at[2], {"row": lax.rem(r + rows - 1, rows)})
    for e in range(1, inner):
        mail.push(xown(1), xpart(r, 1), x_sem.at[r, 1], row_of(zi, turn_x(e)))

    def split(v, left, right, at):
        t = jnp.concatenate([v[:, half:], v[:, :half]], axis=1)
        left[at] = jnp.where(isl, v, none)
        left[at + 1] = jnp.where(isl, t, none)
        right[at] = jnp.where(isl, none, t)
        right[at + 1] = jnp.where(isl, none, v)

    def widen(v, table, at):
        t = jnp.concatenate([v[:, half:], v[:, :half]], axis=1)
        table[at] = jnp.where(isl, v, t)
        table[at + 1] = jnp.where(isl, t, v)

    def each_pack(act):
        for m in range(packs):
            act(m)

    def own_fill(m):
        split(xc_own[m], xl, xr, 2 * (r * packs + m))
        split(xp_own[m], ql, qr, 2 * (packs + m))
        widen(w_own[0, m], wc, 2 * (c * packs + m))
        widen(w_own[1, m], wp, 2 * (c * packs + m))

    each_pack(own_fill)

    me = r * cols + c
    for e in range(1, cols):
        o = lax.rem(c + e, cols)
        mail.landed(na.at[o], na_sem.at[o], near_col)
    na[c] = n_own[...]
    vals = [na[i].astype(F32) for i in range(cols)]
    level = 0
    while len(vals) > 1:
        own = c >> level
        sib_ref[level] = pick(vals, own + 1 - 2 * lax.rem(own, 2)).astype(BF)
        off = dev_count - (dev_count >> level)
        count = len(vals) // 2
        vals = [
            combine(vals[2 * i], vals[2 * i + 1], chunk_at(fv_ref, off + r * count + i, wide),
                    chunk_at(fu_ref, off + r * count + i, wide), ml, mr, isl, half).astype(F32)
            for i in range(count)
        ]
        level += 1
    base_level = level
    top = [vals[0]]

    def ask(t):
        nb[2 * t] = top[0].astype(BF)
        mail.push(nb.at[2 * t], nb.at[2 * t + 1], nb_sem.at[t], {"row": r + (1 << t) * (1 - 2 * lax.rem(r >> t, 2))})

    def answer(t):
        mail.landed(nb.at[2 * t + 1], nb_sem.at[t], near_row)
        lev = base_level + t
        sib_ref[lev] = nb[2 * t + 1]
        if dev_count >> (lev + 1) > 1:
            other = nb[2 * t + 1].astype(F32)
            even = lax.rem(r >> t, 2) == 0
            lo = jnp.where(even, top[0], other)
            hi = jnp.where(even, other, top[0])
            at = dev_count - (dev_count >> lev) + ((me >> lev) >> 1)
            top[0] = combine(lo, hi, chunk_at(fv_ref, at, wide), chunk_at(fu_ref, at, wide), ml, mr, isl, half).astype(F32)
            ask(t + 1)

    row_levels = rows.bit_length() - 1
    ask(0)

    def relay_across():
        for e in range(1, inner):
            o = zi * inner + turn_x(e)
            mail.landed(xpart(o, 0), x_sem.at[o, 0], near_row)
            mail.push(xpart(o, 0), xpart(o, 0), x_sem.at[o, 0], row_of(zi + 1, xi), up)
            mail.push(xpart(o, 0), xpart(o, 0), x_sem.at[o, 0], row_of(zi - 1, xi), down)

    def relay_along(d, e, part):
        for back in (True, False):
            have = zi >= d if back else zi + d < deep
            oz = zi - d if back else zi + d
            o = oz * inner + turn_x(e)
            guarded(have, lambda o=o: mail.landed(xpart(o, part), x_sem.at[o, part], near_row))
            if d < deep - 1:
                onward = jnp.logical_and(have, up if back else down)
                mail.push(xpart(o, part), xpart(o, part), x_sem.at[o, part], row_of(zi + 1 if back else zi - 1, xi), onward)
            if part == 1:
                for f in range(1, inner):
                    mail.push(xpart(o, 1), xpart(o, 1), x_sem.at[o, 1], row_of(zi, turn_x(f)), have)

    def relay_points():
        if inner == 2:
            got = 2 * (1 - xi)
            mail.landed(xp.at[got], p_sem.at[got], near_row)
            to = lax.rem(zi + deep + 1 - 2 * xi, deep)
            mail.push(xp.at[got], xp.at[2 * xi], p_sem.at[2 * xi], row_of(to, xi))

    def relay_w(kind):
        for e in range(1, outer):
            o = lax.rem(oi + e, outer) * 2 + ki
            mail.landed(wa.at[o, kind], w_sem.at[o, kind], near_col)
            mail.push(wa.at[o, kind], wa.at[o, kind], w_sem.at[o, kind], {"col": oi * 2 + 1 - ki})

    def fill_w(kind, table):
        for e in range(outer):
            o = lax.rem(oi + e, outer) * 2 + 1 - ki
            mail.landed(wa.at[o, kind], w_sem.at[o, kind], near_col)
        for e in range(1, cols):
            o = lax.rem(c + e, cols)
            each_pack(lambda m, o=o: widen(wa[o, kind, m], table, 2 * (o * packs + m)))

    def fill_p():
        if inner == 2:
            mail.landed(xp.at[2 * xi], p_sem.at[2 * xi], near_row)
        else:
            mail.landed(xp.at[0], p_sem.at[0], near_row)
            mail.landed(xp.at[2], p_sem.at[2], near_row)
        for k in (0, 2):
            each_pack(lambda m, k=k: split(xp[k, m], ql, qr, 2 * (k * packs + m)))

    def products(pairs, mat, near, side, tables, out, piece, pieces):
        total = out.shape[0] // unroll
        def step(g, carry):
            for k in range(unroll):
                p = g * unroll + k
                i0, i1, j0, j1 = place(pairs, p)
                blk = mat[:, pl.ds(pl.multiple_of(p * wide, wide), wide)]
                if side == "z":
                    if not near:
                        reach = jnp.where(2 * p + 1 < live, wide, jnp.where(2 * p < live, half, 0))
                        blk = jnp.where(lane < reach, blk, none)
                    pair = jnp.concatenate([jnp.where(isl, blk, none), jnp.where(isl, none, blk)], axis=0)
                    out[p] = mm(jnp.where(isl, tables[i0], tables[i1]), pair)
                else:
                    out[p] = mm(blk, jnp.concatenate([tables[0][j0], tables[1][j1]], axis=0))
            return carry
        lax.fori_loop(piece * total // pieces, (piece + 1) * total // pieces, step, 0)

    def near_z(k, n):
        products((ni_ref, nj_ref), d_ref, True, "z", wp, pzn, k, n)

    def far_z(k, n):
        products((fi_ref, fj_ref), s_ref, False, "z", wc, pzc, k, n)

    def near_y(k, n):
        products((ni_ref, nj_ref), d_ref, True, "y", (ql, qr), pyn, k, n)

    relay_across()
    relay_along(1, 0, 1)
    relay_along(1, 0, 0)
    relay_w(1)
    answer(0)
    relay_points()
    fill_w(1, wp)
    near_z(0, 2)
    for e in range(1, inner):
        relay_along(1, e, 0)
    near_z(1, 2)
    for d in range(2, deep):
        relay_along(d, 0, 1)
        relay_along(d, 0, 0)
        if d == 2:
            relay_w(0)
            if row_levels > 1:
                answer(1)
            fill_w(0, wc)
        far_z(d - 2, 2 * (deep - 2))
        for e in range(1, inner):
            relay_along(d, e, 0)
        if d == 2:
            fill_p()
    if deep <= 2:
        relay_w(0)
        fill_w(0, wc)
        fill_p()
        far_z(0, 1)
    else:
        far_z(1, 2)
    near_y(0, 1)
    for t in range(2 if deep > 2 else 1, row_levels):
        answer(t)
    for e in range(1, inner):
        for dz in range(deep):
            o = lax.rem(zi + dz, deep) * inner + turn_x(e)
            mail.landed(xpart(o, 1), x_sem.at[o, 1], near_row)

    def fill_x(i, carry):
        o = lax.rem(r + i, rows)
        for m in range(packs):
            split(xc[o, m], xl, xr, 2 * (o * packs + m))
        return carry

    lax.fori_loop(1, rows, fill_x, 0)
    mail.close()


def pick(vals, at):
    out = vals[0]
    for i in range(1, len(vals)):
        out = jnp.where(at == i, vals[i], out)
    return out


def grant(own, operands):
    mib = 1024 * 1024
    return own // mib + 5 if own + operands < 40 * mib else min(62, (own + operands) // mib + 6)


def slot_kernel(rows, cols, unroll, fi_ref, fj_ref, ni_ref, nj_ref, live_ref, xl, xr, pyn, pzn, pzc, s_ref, y_ref, z_ref, n_ref,
                yc, yn, zc, zn, y0, y1):
    _, q, wide = xl.shape
    half = wide // 2
    packs = z_ref.shape[1]
    leaves = 2 * packs
    live = live_ref[0]
    isl = lax.broadcasted_iota(jnp.int32, (q, wide), 1) < half
    lane = lax.broadcasted_iota(jnp.int32, (q, wide), 1)
    none = jnp.zeros((q, wide), BF)
    blank = jnp.zeros((q, wide), F32)

    def clear(acc):
        group = 8
        def step(i, carry):
            for k in range(group):
                acc[i * group + k] = blank
            return carry
        lax.fori_loop(0, acc.shape[0] // group, step, 0)

    for acc in (yc, yn, zc, zn):
        clear(acc)

    def settle(pairs, p, yv, zv, ya, za):
        i0, i1, j0, j1 = place(pairs, p)
        a = ya[i0, :, :half] + yv[:, :half]
        b = ya[i1, :, half:] + yv[:, half:]
        c = za[j0, :, :half] + zv[:, :half]
        d = za[j1, :, half:] + zv[:, half:]
        ya[i0, :, :half] = a
        ya[i1, :, half:] = b
        za[j0, :, :half] = c
        za[j1, :, half:] = d

    def near_step(g, carry):
        for k in range(unroll):
            p = g * unroll + k
            settle((ni_ref, nj_ref), p, pyn[p], pzn[p], yn, zn)
        return carry

    lax.fori_loop(0, ni_ref.shape[1] // (2 * unroll), near_step, 0)

    def far(g, buf):
        for k in range(unroll):
            p = g * unroll + k
            settle((fi_ref, fj_ref), p, buf[k], pzc[p], yc, zc)

    def multiply(g, buf):
        for k in range(unroll):
            p = g * unroll + k
            j0, j1 = fj_ref[0, 2 * p], fj_ref[0, 2 * p + 1]
            blk = s_ref[:, pl.ds(pl.multiple_of(p * wide, wide), wide)]
            reach = jnp.where(2 * p + 1 < live, wide, jnp.where(2 * p < live, half, 0))
            blk = jnp.where(lane < reach, blk, none)
            top = xl[j0]
            bot = xr[j1]
            pair = jnp.concatenate([top, bot], axis=0)
            buf[k] = mm(blk, pair)

    steps = quot(live + 4 * unroll - 1, 4 * unroll)
    multiply(0, y0)
    def step(g, carry):
        multiply(2 * g + 1, y1)
        far(2 * g, y0)
        multiply(2 * g + 2, y0)
        far(2 * g + 1, y1)
        return carry
    lax.fori_loop(0, steps - 1, step, 0)
    multiply(2 * steps - 1, y1)
    far(2 * steps - 2, y0)
    far(2 * steps - 1, y1)

    def fold(acc, at):
        a, b = acc[at], acc[at + 1]
        return (jnp.where(isl, a, b) + pltpu.roll(jnp.where(isl, b, a), half, 1)).astype(BF)

    def out_y(i, carry):
        for kind, acc in enumerate((yc, yn)):
            for m in range(packs):
                y_ref[i, kind, m] = fold(acc, 2 * (i * packs + m))
        return carry

    def out_z(i, carry):
        for m in range(packs):
            z_ref[i, m] = fold(zc, 2 * (i * packs + m))
        return carry

    def out_n(i, carry):
        for m in range(packs):
            n_ref[i, m] = fold(zn, 2 * (i * packs + m))
        return carry

    lax.fori_loop(0, cols, out_y, 0)
    lax.fori_loop(0, rows, out_z, 0)
    lax.fori_loop(0, 3, out_n, 0)


def down_kernel(rows, cols, y_ref, z_ref, n_ref, sib_ref, order_ref, u_ref, v_ref, eu_ref, ev_ref, fu_ref, fv_ref,
                s_ref, o_ref, y_in, z1_in, z1_out, z2_in, zn_in, y_sem, z1_sem, z2_sem, n_sem):
    _, packs, q, wide = z_ref.shape
    half = wide // 2
    deep, inner = grid_of(rows)
    dev_count = rows * cols
    r = lax.axis_index("row")
    c = lax.axis_index("col")
    me = r * cols + c
    zi = r // inner
    xi = lax.rem(r, inner)
    bar = greet(rows, cols, r, c)
    ml, mr = left_mask(half, BF)
    isl = lax.broadcasted_iota(jnp.int32, (q, wide), 1) < half
    hot = one_hot(order_ref, me * order_ref.shape[1])
    eye = twin_eye(half)
    pl.semaphore_wait(bar, rows + cols - 2)
    first = {}
    for d in list(range(1, deep)) + [0]:
        to = lax.rem(zi + d, deep) * inner
        first[d] = []
        for e in range(1, inner):
            peer = lax.rem(xi + e, inner)
            first[d].append(
                push(z_ref.at[to + peer], z1_in.at[d, e - 1], z1_sem, (d, e - 1), "row", zi * inner + peer)
            )
    near = [
        push(n_ref.at[0], zn_in.at[0], n_sem, (0,), "row", lax.rem(r + rows - 1, rows)),
        push(n_ref.at[2], zn_in.at[1], n_sem, (1,), "row", lax.rem(r + 1, rows)),
    ]
    y_copies = []
    for d in range(1, cols):
        peer = lax.rem(c + d, cols)
        y_copies.append(push(y_ref.at[peer], y_in.at[d - 1], y_sem, (d - 1,), "col", peer))

    second = []
    for d in range(1, deep):
        for copy in first[d]:
            copy.wait_recv()
        to = lax.rem(zi + d, deep) * inner + xi
        for m in range(packs):
            total = z_ref[to, m].astype(F32)
            for e in range(inner - 1):
                total = total + z1_in[d, e, m].astype(F32)
            z1_out[d - 1, m] = total.astype(BF)
        second.append(push(z1_out.at[d - 1], z2_in.at[d - 1], z2_sem, (d - 1,), "row", to))

    levels = dev_count.bit_length() - 1
    lane_half = (lax.broadcasted_iota(jnp.int32, (q, wide), 1) >= half).astype(jnp.int32)

    def turned(v, chunk, side):
        return mm2(jnp.where(lane_half == side, v, 0.0), jnp.concatenate([chunk, chunk], axis=0), NT)

    y_down = z_down = None
    for level in range(levels - 1, -1, -1):
        own = me >> level
        side = lax.rem(own, 2)
        sib = sib_ref[level].astype(F32)
        rolled = pltpu.roll(sib, half, 1)
        xs = jnp.where(isl, sib, rolled)
        ws = jnp.where(isl, rolled, 0.0).astype(BF)
        at = dev_count - (dev_count >> level) + own // 2
        cup = chunk_at(s_ref, at, wide)
        dup = jnp.concatenate([cup, cup], axis=0)
        y_term = mm(jnp.where(lane_half == side, xs, 0.0).astype(BF), dup, NT)
        z_raw = jnp.where(lane_half == 1 - side, mm(ws, dup), 0.0)
        z_term = z_raw + pltpu.roll(z_raw, half, 1)
        if level < levels - 1:
            y_term = y_term + turned(y_down, chunk_at(fu_ref, at, wide), side)
            z_term = z_term + turned(z_down, chunk_at(fv_ref, at, wide), side)
        y_down, z_down = y_term, z_term

    perms = []
    for flip, (down, b_ref, e_ref) in enumerate(((y_down, u_ref, eu_ref), (z_down, v_ref, ev_ref))):
        if flip == 0:
            for copy in y_copies:
                copy.wait_recv()
        else:
            for copy in first[0] + second + near:
                copy.wait_recv()
        parts = []
        for m in range(packs):
            cs = slice(m * wide, (m + 1) * wide)
            if flip == 0:
                coef, raw = y_ref[c, 0, m].astype(F32), y_ref[c, 1, m].astype(F32)
                for d in range(cols - 1):
                    coef = coef + y_in[d, 0, m].astype(F32)
                    raw = raw + y_in[d, 1, m].astype(F32)
            else:
                coef, raw = z_ref[r, m].astype(F32), n_ref[1, m].astype(F32)
                for e in range(inner - 1):
                    coef = coef + z1_in[0, e, m].astype(F32)
                for d in range(deep - 1):
                    coef = coef + z2_in[d, m].astype(F32)
                for k in range(2):
                    raw = raw + zn_in[k, m].astype(F32)
            if flip == 0:
                hi, lo = split2(down)
                e = e_ref[:, cs]
                leaf = (coef + mm(e, diag2(hi, ml, mr), NT) + mm(e, diag2(lo, ml, mr), NT)).astype(BF)
                turned = mm(eye, diag2(b_ref[:, cs], ml, mr), NT).astype(BF)
                pts = (mm(turned, diag2(leaf, ml, mr)) + raw).astype(BF)
                parts.append(mm(eye, diag2(pts, ml, mr), NT).astype(BF))
            else:
                leaf = (coef + mm2(down, diag2(e_ref[:, cs], ml, mr), NT)).astype(BF)
                parts.append((mm(leaf, diag2(b_ref[:, cs], ml, mr)) + raw).astype(BF))
        perms.append(jnp.concatenate(parts, axis=1))
    o_ref[...] = mm(jnp.concatenate(perms, axis=0), hot, NT).astype(BF)
    for copies in (*first.values(), second, near, y_copies):
        for copy in copies:
            copy.wait_send()


def per_device(
    x_vectors,
    w_vectors,
    order,
    ubasis,
    vbasis,
    leaf_up_u,
    leaf_up_v,
    coupling,
    coupling_pairs,
    coupling_count,
    near_blocks,
    near_pairs,
    transfer_u,
    transfer_v,
    upper_coupling,
):
    q, piece = x_vectors.shape
    rank = ubasis.shape[0]
    leaves = leaf_up_u.shape[1] // rank
    packs = leaves // 2
    wide = 2 * rank
    rows = lax.axis_size("row")
    cols = lax.axis_size("col")
    deep, inner = grid_of(rows)
    order2 = order.reshape(1, piece)

    def shape(*lead):
        return jax.ShapeDtypeStruct((*lead, q, wide), BF)

    def wide_shape(*lead):
        return jax.ShapeDtypeStruct((*lead, q, wide), F32)

    def buf(*lead, dtype=BF):
        return pltpu.VMEM((*lead, q, wide), dtype)

    def sems(*lead):
        return pltpu.SemaphoreType.DMA((2, *lead))

    def params(mib, cid=None):
        limit = mib * 1024 * 1024
        if cid is None:
            return pltpu.CompilerParams(vmem_limit_bytes=limit)
        return pltpu.CompilerParams(vmem_limit_bytes=limit, collective_id=cid, has_side_effects=True)

    token = pl.pallas_call(
        first_kernel,
        out_shape=jax.ShapeDtypeStruct((1, wide), F32),
        out_specs=VMEM,
        compiler_params=params(1),
        cost_estimate=pl.CostEstimate(flops=2_000_000_000, bytes_accessed=6_000_000, transcendentals=0),
    )()
    loaded = (token, coupling_pairs, near_pairs, order2, x_vectors, w_vectors, vbasis, ubasis, leaf_up_v, leaf_up_u)
    own_x, own_p, own_w, own_n, *spots = pl.pallas_call(
        local_kernel,
        out_shape=(
            shape(packs), shape(packs), shape(2, packs), shape(),
            *(jax.ShapeDtypeStruct((1, v.shape[1]), jnp.int32) for v in (coupling_pairs, coupling_pairs, near_pairs, near_pairs)),
        ),
        in_specs=[VMEM] * 10,
        out_specs=(VMEM,) * 8,
        compiler_params=params(12),
        cost_estimate=pl.CostEstimate(flops=8_000_000, bytes_accessed=20_000, transcendentals=0),
    )(*loaded)
    unroll = UNROLL
    far_pairs = coupling_pairs.shape[1] // 2
    near_pairs_count = near_pairs.shape[1] // 2
    levels = (rows * cols).bit_length() - 1
    row_levels = rows.bit_length() - 1
    tables = 2 * leaves * (3 + cols)
    raw = packs * (rows + 3 + 2 * cols)
    block = q * wide * 2
    x_left, x_right, p_y, p_z, c_z, sibs = pl.pallas_call(
        functools.partial(gather_kernel, rows, cols, 32),
        out_shape=(
            shape(rows * leaves), shape(rows * leaves), wide_shape(near_pairs_count), wide_shape(near_pairs_count),
            wide_shape(far_pairs), shape(levels),
        ),
        in_specs=[SMEM] * 5 + [VMEM] * 8,
        out_specs=(VMEM,) * 6,
        scratch_shapes=[
            buf(rows, packs),
            buf(3, packs),
            buf(cols, 2, packs),
            buf(cols),
            buf(2 * row_levels),
            buf(3 * leaves),
            buf(3 * leaves),
            buf(cols * leaves),
            buf(cols * leaves),
            pltpu.SemaphoreType.DMA((128,)),
            pltpu.SemaphoreType.DMA((rows, 2)),
            pltpu.SemaphoreType.DMA((3,)),
            pltpu.SemaphoreType.DMA((cols, 2)),
            pltpu.SemaphoreType.DMA((cols,)),
            pltpu.SemaphoreType.DMA((row_levels,)),
        ],
        compiler_params=params(6 + (tables + raw) * block // 1024**2, 0),
        cost_estimate=pl.CostEstimate(flops=20_000_000_000, bytes_accessed=60_000_000, transcendentals=0),
    )(
        *spots, coupling_count, own_x, own_p, own_w, own_n, transfer_u, transfer_v,
        coupling, near_blocks,
    )
    sums = leaves * (2 * cols + rows + 3) + 2 * unroll
    y_part, z_part, n_part = pl.pallas_call(
        functools.partial(slot_kernel, rows, cols, unroll),
        out_shape=(shape(cols, 2, packs), shape(rows, packs), shape(3, packs)),
        in_specs=[SMEM] * 5 + [VMEM] * 6,
        out_specs=(VMEM,) * 3,
        scratch_shapes=[
            buf(cols * leaves, dtype=F32),
            buf(cols * leaves, dtype=F32),
            buf(rows * leaves, dtype=F32),
            buf(3 * leaves, dtype=F32),
            buf(unroll, dtype=F32),
            buf(unroll, dtype=F32),
        ],
        compiler_params=params(grant(sums * 2 * block, 2 * rows * leaves * block + (near_pairs_count * 2 + far_pairs) * 2 * block + far_pairs * wide * q * 2)),
        cost_estimate=pl.CostEstimate(flops=20_000_000_000, bytes_accessed=60_000_000, transcendentals=0),
    )(*spots, coupling_count, x_left, x_right, p_y, p_z, c_z, coupling)
    out = pl.pallas_call(
        functools.partial(down_kernel, rows, cols),
        out_shape=jax.ShapeDtypeStruct((2 * q, piece), BF),
        in_specs=[VMEM] * 12,
        out_specs=VMEM,
        scratch_shapes=[
            buf(cols - 1, 2, packs),
            buf(deep, inner - 1, packs),
            buf(deep - 1, packs),
            buf(deep - 1, packs),
            buf(2, packs),
            sems(cols - 1),
            sems(deep, inner - 1),
            sems(deep - 1),
            sems(2),
        ],
        compiler_params=params(16, 1),
    )(
        y_part, z_part, n_part, sibs, order2, ubasis, vbasis, leaf_up_u, leaf_up_v,
        transfer_u, transfer_v, upper_coupling,
    )
    return out[:q], out[q:]


def solution(mesh):
    both = P(None, ("row", "col"))
    flat = P(("row", "col"))
    return jax.shard_map(
        per_device,
        mesh=mesh,
        in_specs=(both, both, flat, both, both, both, both, both, both, flat, both, both, P(), P(), P()),
        out_specs=(both, both),
        check_vma=False,
    )
```

```python
import functools

import jax
import jax.numpy as jnp
from jax import lax
from jax.experimental import pallas as pl
from jax.experimental.pallas import tpu as pltpu
from jax.sharding import PartitionSpec as P

BF = jnp.bfloat16
F32 = jnp.float32
VMEM = pl.BlockSpec(memory_space=pltpu.VMEM)
SMEM = pl.BlockSpec(memory_space=pltpu.SMEM)
NN = (((1,), (0,)), ((), ()))
NT = (((1,), (1,)), ((), ()))
UNROLL = 8


def mm(a, b, dims=NN):
    return lax.dot_general(a, b, dims, preferred_element_type=F32)


def left_mask(half, dtype):
    lane = lax.broadcasted_iota(jnp.int32, (1, 2 * half), 1)
    return (lane < half).astype(F32).astype(dtype), (lane >= half).astype(F32).astype(dtype)


def diag2(v, ml, mr):
    return jnp.concatenate([v * ml, v * mr], axis=0)


def quot(v, n):
    return lax.shift_right_logical(v, n.bit_length() - 1) if n & (n - 1) == 0 else lax.div(v, n)


def mod(v, n):
    return lax.bitwise_and(v, n - 1) if n & (n - 1) == 0 else lax.rem(v, n)


def split2(v):
    hi = v.astype(BF)
    return hi, (v - hi.astype(F32)).astype(BF)


def mm2(v, b, dims):
    hi, lo = split2(v)
    return mm(hi, b, dims) + mm(lo, b, dims)


def one_hot(order_ref, base):
    n = order_ref.shape[1]
    src = lax.broadcasted_iota(jnp.int32, (n, n), 0)
    return jnp.where(src == order_ref[...] - base, 1.0, 0.0).astype(BF)


def twin_eye(half):
    row = lax.broadcasted_iota(jnp.int32, (half, 2 * half), 0)
    lane = lax.broadcasted_iota(jnp.int32, (half, 2 * half), 1)
    return jnp.where(jnp.logical_or(lane == row, lane == row + half), 1.0, 0.0).astype(BF)


def grid_of(rows):
    inner = 1 << ((rows.bit_length() - 1) // 2)
    return rows // inner, inner


def greet(rows, cols, r, c):
    bar = pltpu.get_barrier_semaphore()
    for d in range(1, rows):
        pl.semaphore_signal(bar, inc=1, device_id={"row": lax.rem(r + d, rows)}, device_id_type=pl.DeviceIdType.MESH)
    for d in range(1, cols):
        pl.semaphore_signal(bar, inc=1, device_id={"col": lax.rem(c + d, cols)}, device_id_type=pl.DeviceIdType.MESH)
    return bar


def push(src, dst, sems, at, axis, peer):
    copy = pltpu.make_async_remote_copy(
        src_ref=src,
        dst_ref=dst,
        send_sem=sems.at[(0, *at)],
        recv_sem=sems.at[(1, *at)],
        device_id={axis: peer},
        device_id_type=pl.DeviceIdType.MESH,
    )
    copy.start()
    return copy


def chunk_at(ref, at, wide):
    return ref[:, pl.ds(pl.multiple_of(at * wide, wide), wide)]


def combine(v0, v1, fv, fu, ml, mr, isl, half):
    xp = jnp.where(isl, v0, pltpu.roll(v1, half, 1)).astype(BF)
    wp = jnp.where(isl, pltpu.roll(v0, half, 1), v1).astype(BF)
    x = mm(xp, diag2(fv, ml, mr))
    w = mm(wp, diag2(fu, ml, mr))
    return jnp.where(isl, x + pltpu.roll(x, half, 1), w + pltpu.roll(w, half, 1)).astype(BF)


def first_kernel(token_ref):
    token_ref[...] = jnp.zeros(token_ref.shape, token_ref.dtype)


def local_kernel(token_ref, far_ref, near_ref, order_ref, x_ref, w_ref, v_ref, u_ref, ev_ref, eu_ref,
                 xc_ref, xp_ref, w_out, n_ref, fi_ref, fj_ref, ni_ref, nj_ref):
    q, n = x_ref.shape
    packs = xc_ref.shape[0]
    wide = xc_ref.shape[2]
    half = wide // 2
    rows, cols = lax.axis_size("row"), lax.axis_size("col")
    my_row = lax.axis_index("row")
    base = (my_row * cols + lax.axis_index("col")) * n
    leaves = 2 * packs
    for pairs, i_ref, j_ref, near in ((far_ref, fi_ref, fj_ref, False), (near_ref, ni_ref, nj_ref, True)):
        leaf = pairs[1:2]
        group = quot(leaf, cols * leaves)
        if near:
            group = mod(group - my_row + (rows + 1), rows)
        i_ref[...] = pairs[0:1] - my_row * cols * leaves
        j_ref[...] = group * leaves + mod(leaf, leaves)
    ml, mr = left_mask(half, BF)
    isl = lax.broadcasted_iota(jnp.int32, (q, wide), 1) < half
    eye = twin_eye(half)
    hot = one_hot(order_ref, base)
    both = mm(jnp.concatenate([x_ref[...], w_ref[...]], axis=0), hot).astype(BF)
    folds = []
    for side, (b_ref, e_ref) in enumerate(((v_ref, ev_ref), (u_ref, eu_ref))):
        pts = both[side * q:(side + 1) * q]
        node = jnp.zeros((q, wide), F32)
        for m in range(packs):
            cs = slice(m * wide, (m + 1) * wide)
            pm = pts[:, cs]
            cm = mm(pm, diag2(b_ref[:, cs], ml, mr), NT).astype(BF)
            if side == 0:
                turned = diag2(pm, ml, mr)
                xc_ref[m] = mm(b_ref[:, cs], turned, NT).astype(BF)
                xp_ref[m] = mm(eye, turned, NT).astype(BF)
            else:
                w_out[0, m] = cm
                w_out[1, m] = pm
            node = node + mm(cm, diag2(e_ref[:, cs], ml, mr))
        folds.append(node + pltpu.roll(node, half, 1))
    n_ref[...] = jnp.where(isl, folds[0], folds[1]).astype(BF)


class Mail:
    def __init__(self, sem):
        self.sem = sem
        self.sent = []

    def copy(self, src, dst, recv, peer, at):
        return pltpu.make_async_remote_copy(
            src_ref=src,
            dst_ref=dst,
            send_sem=self.sem.at[at],
            recv_sem=recv,
            device_id=peer,
            device_id_type=pl.DeviceIdType.MESH,
        )

    def push(self, src, dst, recv, peer, when=None):
        args = (src, dst, recv, peer, len(self.sent))
        self.sent.append((args, when))
        guarded(when, lambda: self.copy(*args).start())

    def landed(self, dst, recv, peer):
        self.copy(dst, dst, recv, peer, 0).wait_recv()

    def close(self):
        for args, when in self.sent:
            guarded(when, lambda args=args: self.copy(*args).wait_send())


def guarded(when, act):
    if when is None:
        act()
    else:
        pl.when(when)(act)


def place(pairs, p):
    i_ref, j_ref = pairs
    return i_ref[0, 2 * p], i_ref[0, 2 * p + 1], j_ref[0, 2 * p], j_ref[0, 2 * p + 1]


def gather_kernel(rows, cols, unroll, fi_ref, fj_ref, ni_ref, nj_ref, live_ref, xc_own, xp_own, w_own, n_own, fu_ref, fv_ref, s_ref, d_ref,
                  xl, xr, pyn, pzn, pzc, sib_ref,
                  xc, xp, wa, na, nb, ql, qr, wc, wp, send_sem, x_sem, p_sem, w_sem, na_sem, nb_sem):
    packs, q, wide = xc_own.shape
    half = wide // 2
    leaves = 2 * packs
    deep, inner = grid_of(rows)
    outer = cols // 2
    dev_count = rows * cols
    first = (1 * packs) // 8
    cuts = ((0, first), (first, packs - first))
    r = lax.axis_index("row")
    c = lax.axis_index("col")
    zi = r // inner
    xi = lax.rem(r, inner)
    oi = c // 2
    ki = lax.rem(c, 2)
    live = live_ref[0]
    bar = greet(rows, cols, r, c)
    ml, mr = left_mask(half, BF)
    isl = lax.broadcasted_iota(jnp.int32, (q, wide), 1) < half
    lane = lax.broadcasted_iota(jnp.int32, (q, wide), 1)
    none = jnp.zeros((q, wide), BF)
    mail = Mail(send_sem)
    near_row = {"row": lax.rem(r + 1, rows)}
    near_col = {"col": lax.rem(c + 1, cols)}

    def row_of(z, x):
        return {"row": z * inner + x}

    def turn_x(e):
        return lax.rem(xi + e, inner)

    def xpart(row, part):
        return xc.at[row, pl.ds(*cuts[part])]

    def xown(part):
        return xc_own.at[pl.ds(*cuts[part])]

    up, down = zi < deep - 1, zi > 0
    pl.semaphore_wait(bar, rows + cols - 2)

    for e in range(1, cols):
        mail.push(n_own, na.at[c], na_sem.at[c], {"col": lax.rem(c + e, cols)})
    for kind in (1, 0):
        for e in range(1, outer):
            mail.push(w_own.at[kind], wa.at[c, kind], w_sem.at[c, kind], {"col": lax.rem(oi + e, outer) * 2 + ki})
        mail.push(w_own.at[kind], wa.at[c, kind], w_sem.at[c, kind], {"col": oi * 2 + 1 - ki})
    for e in range(1, inner):
        mail.push(xown(0), xpart(r, 0), x_sem.at[r, 0], row_of(zi, turn_x(e)))
    for part in (1, 0):
        mail.push(xown(part), xpart(r, part), x_sem.at[r, part], row_of(zi + 1, xi), up)
        mail.push(xown(part), xpart(r, part), x_sem.at[r, part], row_of(zi - 1, xi), down)
    if inner == 2:
        mail.push(xp_own, xp.at[2 * xi], p_sem.at[2 * xi], row_of(zi, 1 - xi))
    else:
        mail.push(xp_own, xp.at[0], p_sem.at[0], {"row": lax.rem(r + 1, rows)})
        mail.push(xp_own, xp.at[2], p_sem.at[2], {"row": lax.rem(r + rows - 1, rows)})
    for e in range(1, inner):
        mail.push(xown(1), xpart(r, 1), x_sem.at[r, 1], row_of(zi, turn_x(e)))

    def split(v, left, right, at):
        t = jnp.concatenate([v[:, half:], v[:, :half]], axis=1)
        left[at] = jnp.where(isl, v, none)
        left[at + 1] = jnp.where(isl, t, none)
        right[at] = jnp.where(isl, none, t)
        right[at + 1] = jnp.where(isl, none, v)

    def widen(v, table, at):
        t = jnp.concatenate([v[:, half:], v[:, :half]], axis=1)
        table[at] = jnp.where(isl, v, t)
        table[at + 1] = jnp.where(isl, t, v)

    def each_pack(act):
        for m in range(packs):
            act(m)

    def own_fill(m):
        split(xc_own[m], xl, xr, 2 * (r * packs + m))
        split(xp_own[m], ql, qr, 2 * (packs + m))
        widen(w_own[0, m], wc, 2 * (c * packs + m))
        widen(w_own[1, m], wp, 2 * (c * packs + m))

    each_pack(own_fill)

    me = r * cols + c
    for e in range(1, cols):
        o = lax.rem(c + e, cols)
        mail.landed(na.at[o], na_sem.at[o], near_col)
    na[c] = n_own[...]
    vals = [na[i].astype(F32) for i in range(cols)]
    level = 0
    while len(vals) > 1:
        own = c >> level
        sib_ref[level] = pick(vals, own + 1 - 2 * lax.rem(own, 2)).astype(BF)
        off = dev_count - (dev_count >> level)
        count = len(vals) // 2
        vals = [
            combine(vals[2 * i], vals[2 * i + 1], chunk_at(fv_ref, off + r * count + i, wide),
                    chunk_at(fu_ref, off + r * count + i, wide), ml, mr, isl, half).astype(F32)
            for i in range(count)
        ]
        level += 1
    base_level = level
    top = [vals[0]]

    def ask(t):
        nb[2 * t] = top[0].astype(BF)
        mail.push(nb.at[2 * t], nb.at[2 * t + 1], nb_sem.at[t], {"row": r + (1 << t) * (1 - 2 * lax.rem(r >> t, 2))})

    def answer(t):
        mail.landed(nb.at[2 * t + 1], nb_sem.at[t], near_row)
        lev = base_level + t
        sib_ref[lev] = nb[2 * t + 1]
        if dev_count >> (lev + 1) > 1:
            other = nb[2 * t + 1].astype(F32)
            even = lax.rem(r >> t, 2) == 0
            lo = jnp.where(even, top[0], other)
            hi = jnp.where(even, other, top[0])
            at = dev_count - (dev_count >> lev) + ((me >> lev) >> 1)
            top[0] = combine(lo, hi, chunk_at(fv_ref, at, wide), chunk_at(fu_ref, at, wide), ml, mr, isl, half).astype(F32)
            ask(t + 1)

    row_levels = rows.bit_length() - 1
    ask(0)

    def relay_across():
        for e in range(1, inner):
            o = zi * inner + turn_x(e)
            mail.landed(xpart(o, 0), x_sem.at[o, 0], near_row)
            mail.push(xpart(o, 0), xpart(o, 0), x_sem.at[o, 0], row_of(zi + 1, xi), up)
            mail.push(xpart(o, 0), xpart(o, 0), x_sem.at[o, 0], row_of(zi - 1, xi), down)

    def relay_along(d, e, part):
        for back in (True, False):
            have = zi >= d if back else zi + d < deep
            oz = zi - d if back else zi + d
            o = oz * inner + turn_x(e)
            guarded(have, lambda o=o: mail.landed(xpart(o, part), x_sem.at[o, part], near_row))
            if d < deep - 1:
                onward = jnp.logical_and(have, up if back else down)
                mail.push(xpart(o, part), xpart(o, part), x_sem.at[o, part], row_of(zi + 1 if back else zi - 1, xi), onward)
            if part == 1:
                for f in range(1, inner):
                    mail.push(xpart(o, 1), xpart(o, 1), x_sem.at[o, 1], row_of(zi, turn_x(f)), have)

    def relay_points():
        if inner == 2:
            got = 2 * (1 - xi)
            mail.landed(xp.at[got], p_sem.at[got], near_row)
            to = lax.rem(zi + deep + 1 - 2 * xi, deep)
            mail.push(xp.at[got], xp.at[2 * xi], p_sem.at[2 * xi], row_of(to, xi))

    def relay_w(kind):
        for e in range(1, outer):
            o = lax.rem(oi + e, outer) * 2 + ki
            mail.landed(wa.at[o, kind], w_sem.at[o, kind], near_col)
            mail.push(wa.at[o, kind], wa.at[o, kind], w_sem.at[o, kind], {"col": oi * 2 + 1 - ki})

    def fill_w(kind, table):
        for e in range(outer):
            o = lax.rem(oi + e, outer) * 2 + 1 - ki
            mail.landed(wa.at[o, kind], w_sem.at[o, kind], near_col)
        for e in range(1, cols):
            o = lax.rem(c + e, cols)
            each_pack(lambda m, o=o: widen(wa[o, kind, m], table, 2 * (o * packs + m)))

    def fill_p():
        if inner == 2:
            mail.landed(xp.at[2 * xi], p_sem.at[2 * xi], near_row)
        else:
            mail.landed(xp.at[0], p_sem.at[0], near_row)
            mail.landed(xp.at[2], p_sem.at[2], near_row)
        for k in (0, 2):
            each_pack(lambda m, k=k: split(xp[k, m], ql, qr, 2 * (k * packs + m)))

    def products(pairs, mat, near, side, tables, out, piece, pieces):
        total = out.shape[0] // unroll
        def step(g, carry):
            for k in range(unroll):
                p = g * unroll + k
                i0, i1, j0, j1 = place(pairs, p)
                blk = mat[:, pl.ds(pl.multiple_of(p * wide, wide), wide)]
                if side == "z":
                    if not near:
                        reach = jnp.where(2 * p + 1 < live, wide, jnp.where(2 * p < live, half, 0))
                        blk = jnp.where(lane < reach, blk, none)
                    pair = jnp.concatenate([jnp.where(isl, blk, none), jnp.where(isl, none, blk)], axis=0)
                    out[p] = mm(jnp.where(isl, tables[i0], tables[i1]), pair)
                else:
                    out[p] = mm(blk, jnp.concatenate([tables[0][j0], tables[1][j1]], axis=0))
            return carry
        lax.fori_loop(piece * total // pieces, (piece + 1) * total // pieces, step, 0)

    def near_z(k, n):
        products((ni_ref, nj_ref), d_ref, True, "z", wp, pzn, k, n)

    def far_z(k, n):
        products((fi_ref, fj_ref), s_ref, False, "z", wc, pzc, k, n)

    def near_y(k, n):
        products((ni_ref, nj_ref), d_ref, True, "y", (ql, qr), pyn, k, n)

    def fill_rows(e):
        def step(dz, carry):
            o = lax.rem(zi + dz, deep) * inner + turn_x(e)
            for m in range(packs):
                split(xc[o, m], xl, xr, 2 * (o * packs + m))
            return carry
        lax.fori_loop(1 if e == 0 else 0, deep, step, 0)

    relay_across()
    relay_along(1, 0, 1)
    relay_along(1, 0, 0)
    for e in range(1, inner):
        relay_along(1, e, 0)
    relay_w(1)
    answer(0)
    fill_w(1, wp)
    near_z(0, 1)
    for d in range(2, deep):
        relay_along(d, 0, 1)
        relay_along(d, 0, 0)
        if d == 2:
            relay_points()
            relay_w(0)
        for e in range(1, inner):
            relay_along(d, e, 0)
        if d == 2:
            if row_levels > 1:
                answer(1)
            fill_w(0, wc)
            far_z(0, 1)
    if deep <= 2:
        relay_points()
        relay_w(0)
        fill_w(0, wc)
        far_z(0, 1)
    fill_rows(0)
    fill_p()
    near_y(0, 1)
    for t in range(2 if deep > 2 else 1, row_levels):
        answer(t)
    for e in range(1, inner):
        for dz in range(deep):
            o = lax.rem(zi + dz, deep) * inner + turn_x(e)
            mail.landed(xpart(o, 1), x_sem.at[o, 1], near_row)
        fill_rows(e)
    mail.close()


def pick(vals, at):
    out = vals[0]
    for i in range(1, len(vals)):
        out = jnp.where(at == i, vals[i], out)
    return out


def grant(own, operands):
    mib = 1024 * 1024
    return own // mib + 5 if own + operands < 40 * mib else min(62, (own + operands) // mib + 6)


def slot_kernel(rows, cols, unroll, fi_ref, fj_ref, ni_ref, nj_ref, live_ref, xl, xr, pyn, pzn, pzc, s_ref, y_ref, z_ref, n_ref,
                yc, yn, zc, zn, y0, y1):
    _, q, wide = xl.shape
    half = wide // 2
    packs = z_ref.shape[1]
    leaves = 2 * packs
    live = live_ref[0]
    isl = lax.broadcasted_iota(jnp.int32, (q, wide), 1) < half
    lane = lax.broadcasted_iota(jnp.int32, (q, wide), 1)
    none = jnp.zeros((q, wide), BF)
    blank = jnp.zeros((q, wide), F32)

    def clear(acc):
        group = 8
        def step(i, carry):
            for k in range(group):
                acc[i * group + k] = blank
            return carry
        lax.fori_loop(0, acc.shape[0] // group, step, 0)

    for acc in (yc, yn, zc, zn):
        clear(acc)

    def settle(pairs, p, yv, zv, ya, za):
        i0, i1, j0, j1 = place(pairs, p)
        a = ya[i0, :, :half] + yv[:, :half]
        b = ya[i1, :, half:] + yv[:, half:]
        c = za[j0, :, :half] + zv[:, :half]
        d = za[j1, :, half:] + zv[:, half:]
        ya[i0, :, :half] = a
        ya[i1, :, half:] = b
        za[j0, :, :half] = c
        za[j1, :, half:] = d

    def near_step(g, carry):
        for k in range(unroll):
            p = g * unroll + k
            settle((ni_ref, nj_ref), p, pyn[p], pzn[p], yn, zn)
        return carry

    lax.fori_loop(0, ni_ref.shape[1] // (2 * unroll), near_step, 0)

    def far(g, buf):
        for k in range(unroll):
            p = g * unroll + k
            settle((fi_ref, fj_ref), p, buf[k], pzc[p], yc, zc)

    def multiply(g, buf):
        for k in range(unroll):
            p = g * unroll + k
            j0, j1 = fj_ref[0, 2 * p], fj_ref[0, 2 * p + 1]
            blk = s_ref[:, pl.ds(pl.multiple_of(p * wide, wide), wide)]
            reach = jnp.where(2 * p + 1 < live, wide, jnp.where(2 * p < live, half, 0))
            blk = jnp.where(lane < reach, blk, none)
            top = xl[j0]
            bot = xr[j1]
            pair = jnp.concatenate([top, bot], axis=0)
            buf[k] = mm(blk, pair)

    steps = quot(live + 4 * unroll - 1, 4 * unroll)
    multiply(0, y0)
    def step(g, carry):
        multiply(2 * g + 1, y1)
        far(2 * g, y0)
        multiply(2 * g + 2, y0)
        far(2 * g + 1, y1)
        return carry
    lax.fori_loop(0, steps - 1, step, 0)
    multiply(2 * steps - 1, y1)
    far(2 * steps - 2, y0)
    far(2 * steps - 1, y1)

    def fold(acc, at):
        a, b = acc[at], acc[at + 1]
        return (jnp.where(isl, a, b) + pltpu.roll(jnp.where(isl, b, a), half, 1)).astype(BF)

    def out_y(i, carry):
        for kind, acc in enumerate((yc, yn)):
            for m in range(packs):
                y_ref[i, kind, m] = fold(acc, 2 * (i * packs + m))
        return carry

    def out_z(i, carry):
        for m in range(packs):
            z_ref[i, m] = fold(zc, 2 * (i * packs + m))
        return carry

    def out_n(i, carry):
        for m in range(packs):
            n_ref[i, m] = fold(zn, 2 * (i * packs + m))
        return carry

    lax.fori_loop(0, cols, out_y, 0)
    lax.fori_loop(0, rows, out_z, 0)
    lax.fori_loop(0, 3, out_n, 0)


def down_kernel(rows, cols, y_ref, z_ref, n_ref, sib_ref, order_ref, u_ref, v_ref, eu_ref, ev_ref, fu_ref, fv_ref,
                s_ref, o_ref, y_in, z1_in, z1_out, z2_in, zn_in, zn_out, ahead_y, ahead_z, u_turn, hot_turn,
                y_sem, z1_sem, z2_sem, n_sem):
    _, packs, q, wide = z_ref.shape
    half = wide // 2
    deep, inner = grid_of(rows)
    dev_count = rows * cols
    r = lax.axis_index("row")
    c = lax.axis_index("col")
    me = r * cols + c
    zi = r // inner
    xi = lax.rem(r, inner)
    bar = greet(rows, cols, r, c)
    ml, mr = left_mask(half, BF)
    isl = lax.broadcasted_iota(jnp.int32, (q, wide), 1) < half
    eye = twin_eye(half)
    pl.semaphore_wait(bar, rows + cols - 2)
    folded = inner == 2
    if folded:
        to = lax.rem(zi + deep - 1 + 2 * xi, deep) * inner + xi
        near = [push(n_ref.at[2 * xi], zn_in.at[0], n_sem, (0,), "row", to)]
    else:
        near = [
            push(n_ref.at[0], zn_in.at[0], n_sem, (0,), "row", lax.rem(r + rows - 1, rows)),
            push(n_ref.at[2], zn_in.at[1], n_sem, (1,), "row", lax.rem(r + 1, rows)),
        ]
    first = {}
    for d in list(range(1, deep)) + [0]:
        to = lax.rem(zi + d, deep) * inner
        first[d] = []
        for e in range(1, inner):
            peer = lax.rem(xi + e, inner)
            first[d].append(
                push(z_ref.at[to + peer], z1_in.at[d, e - 1], z1_sem, (d, e - 1), "row", zi * inner + peer)
            )
    y_copies = []
    for d in range(1, cols):
        peer = lax.rem(c + d, cols)
        y_copies.append(push(y_ref.at[peer], y_in.at[d - 1], y_sem, (d - 1,), "col", peer))

    levels = dev_count.bit_length() - 1
    lane_half = (lax.broadcasted_iota(jnp.int32, (q, wide), 1) >= half).astype(jnp.int32)

    def turned(v, chunk, side):
        return mm2(jnp.where(lane_half == side, v, 0.0), jnp.concatenate([chunk, chunk], axis=0), NT)

    y_down = z_down = None
    for level in range(levels - 1, -1, -1):
        own = me >> level
        side = lax.rem(own, 2)
        sib = sib_ref[level].astype(F32)
        rolled = pltpu.roll(sib, half, 1)
        xs = jnp.where(isl, sib, rolled)
        ws = jnp.where(isl, rolled, 0.0).astype(BF)
        at = dev_count - (dev_count >> level) + own // 2
        cup = chunk_at(s_ref, at, wide)
        dup = jnp.concatenate([cup, cup], axis=0)
        y_term = mm(jnp.where(lane_half == side, xs, 0.0).astype(BF), dup, NT)
        z_raw = jnp.where(lane_half == 1 - side, mm(ws, dup), 0.0)
        z_term = z_raw + pltpu.roll(z_raw, half, 1)
        if level < levels - 1:
            y_term = y_term + turned(y_down, chunk_at(fu_ref, at, wide), side)
            z_term = z_term + turned(z_down, chunk_at(fv_ref, at, wide), side)
        y_down, z_down = y_term, z_term

    second = []

    def pass_on(d):
        for copy in first[d]:
            copy.wait_recv()
        to = lax.rem(zi + d, deep) * inner + xi
        for m in range(packs):
            total = z_ref[to, m].astype(F32)
            for e in range(inner - 1):
                total = total + z1_in[d, e, m].astype(F32)
            z1_out[d - 1, m] = total.astype(BF)
        second.append(push(z1_out.at[d - 1], z2_in.at[d - 1], z2_sem, (d - 1,), "row", to))

    def pass_near():
        if folded:
            near[0].wait_recv()
            for m in range(packs):
                zn_out[m] = (zn_in[0, m].astype(F32) + n_ref[2 * (1 - xi), m].astype(F32)).astype(BF)
            near.append(push(zn_out, zn_in.at[1], n_sem, (1,), "row", zi * inner + 1 - xi))

    def columns(m):
        return slice(m * wide, (m + 1) * wide)

    if deep > 1:
        pass_on(1)
    pass_near()
    hi, lo = split2(y_down)
    hi, lo = diag2(hi, ml, mr), diag2(lo, ml, mr)
    for m in range(packs):
        e = eu_ref[:, columns(m)]
        ahead_y[m] = mm(e, hi, NT) + mm(e, lo, NT)
        ahead_z[m] = mm2(z_down, diag2(ev_ref[:, columns(m)], ml, mr), NT)
        u_turn[m] = mm(eye, diag2(u_ref[:, columns(m)], ml, mr), NT).astype(BF)
    if deep > 2:
        pass_on(2)
    hot_turn[...] = jnp.transpose(one_hot(order_ref, me * order_ref.shape[1]))
    for d in range(3, deep):
        pass_on(d)

    for copy in y_copies:
        copy.wait_recv()
    parts = []
    for m in range(packs):
        coef, raw = y_ref[c, 0, m].astype(F32), y_ref[c, 1, m].astype(F32)
        for d in range(cols - 1):
            coef = coef + y_in[d, 0, m].astype(F32)
            raw = raw + y_in[d, 1, m].astype(F32)
        leaf = (coef + ahead_y[m]).astype(BF)
        pts = (mm(u_turn[m], diag2(leaf, ml, mr)) + raw).astype(BF)
        parts.append(mm(eye, diag2(pts, ml, mr), NT).astype(BF))
    o_ref[:q] = mm(jnp.concatenate(parts, axis=1), hot_turn[...]).astype(BF)

    for copy in first[0] + second + near[1 if folded else 0:]:
        copy.wait_recv()
    parts = []
    for m in range(packs):
        coef, raw = z_ref[r, m].astype(F32), n_ref[1, m].astype(F32)
        for e in range(inner - 1):
            coef = coef + z1_in[0, e, m].astype(F32)
        for d in range(deep - 1):
            coef = coef + z2_in[d, m].astype(F32)
        for k in ((1,) if folded else (0, 1)):
            raw = raw + zn_in[k, m].astype(F32)
        leaf = (coef + ahead_z[m]).astype(BF)
        parts.append((mm(leaf, diag2(v_ref[:, columns(m)], ml, mr)) + raw).astype(BF))
    o_ref[q:] = mm(jnp.concatenate(parts, axis=1), hot_turn[...]).astype(BF)
    for copies in (*first.values(), second, near, y_copies):
        for copy in copies:
            copy.wait_send()


def per_device(
    x_vectors,
    w_vectors,
    order,
    ubasis,
    vbasis,
    leaf_up_u,
    leaf_up_v,
    coupling,
    coupling_pairs,
    coupling_count,
    near_blocks,
    near_pairs,
    transfer_u,
    transfer_v,
    upper_coupling,
):
    q, piece = x_vectors.shape
    rank = ubasis.shape[0]
    leaves = leaf_up_u.shape[1] // rank
    packs = leaves // 2
    wide = 2 * rank
    rows = lax.axis_size("row")
    cols = lax.axis_size("col")
    deep, inner = grid_of(rows)
    order2 = order.reshape(1, piece)

    def shape(*lead):
        return jax.ShapeDtypeStruct((*lead, q, wide), BF)

    def wide_shape(*lead):
        return jax.ShapeDtypeStruct((*lead, q, wide), F32)

    def buf(*lead, dtype=BF):
        return pltpu.VMEM((*lead, q, wide), dtype)

    def sems(*lead):
        return pltpu.SemaphoreType.DMA((2, *lead))

    def params(mib, cid=None):
        limit = mib * 1024 * 1024
        if cid is None:
            return pltpu.CompilerParams(vmem_limit_bytes=limit)
        return pltpu.CompilerParams(vmem_limit_bytes=limit, collective_id=cid, has_side_effects=True)

    token = pl.pallas_call(
        first_kernel,
        out_shape=jax.ShapeDtypeStruct((1, wide), F32),
        out_specs=VMEM,
        compiler_params=params(1),
        cost_estimate=pl.CostEstimate(flops=2_000_000_000, bytes_accessed=6_000_000, transcendentals=0),
    )()
    loaded = (token, coupling_pairs, near_pairs, order2, x_vectors, w_vectors, vbasis, ubasis, leaf_up_v, leaf_up_u)
    own_x, own_p, own_w, own_n, *spots = pl.pallas_call(
        local_kernel,
        out_shape=(
            shape(packs), shape(packs), shape(2, packs), shape(),
            *(jax.ShapeDtypeStruct((1, v.shape[1]), jnp.int32) for v in (coupling_pairs, coupling_pairs, near_pairs, near_pairs)),
        ),
        in_specs=[VMEM] * 10,
        out_specs=(VMEM,) * 8,
        compiler_params=params(12),
        cost_estimate=pl.CostEstimate(flops=8_000_000, bytes_accessed=20_000, transcendentals=0),
    )(*loaded)
    unroll = UNROLL
    far_pairs = coupling_pairs.shape[1] // 2
    near_pairs_count = near_pairs.shape[1] // 2
    levels = (rows * cols).bit_length() - 1
    row_levels = rows.bit_length() - 1
    tables = 2 * leaves * (3 + cols)
    raw = packs * (rows + 3 + 2 * cols)
    block = q * wide * 2
    x_left, x_right, p_y, p_z, c_z, sibs = pl.pallas_call(
        functools.partial(gather_kernel, rows, cols, 32),
        out_shape=(
            shape(rows * leaves), shape(rows * leaves), wide_shape(near_pairs_count), wide_shape(near_pairs_count),
            wide_shape(far_pairs), shape(levels),
        ),
        in_specs=[SMEM] * 5 + [VMEM] * 8,
        out_specs=(VMEM,) * 6,
        scratch_shapes=[
            buf(rows, packs),
            buf(3, packs),
            buf(cols, 2, packs),
            buf(cols),
            buf(2 * row_levels),
            buf(3 * leaves),
            buf(3 * leaves),
            buf(cols * leaves),
            buf(cols * leaves),
            pltpu.SemaphoreType.DMA((128,)),
            pltpu.SemaphoreType.DMA((rows, 2)),
            pltpu.SemaphoreType.DMA((3,)),
            pltpu.SemaphoreType.DMA((cols, 2)),
            pltpu.SemaphoreType.DMA((cols,)),
            pltpu.SemaphoreType.DMA((row_levels,)),
        ],
        compiler_params=params(6 + (tables + raw) * block // 1024**2, 0),
        cost_estimate=pl.CostEstimate(flops=20_000_000_000, bytes_accessed=60_000_000, transcendentals=0),
    )(
        *spots, coupling_count, own_x, own_p, own_w, own_n, transfer_u, transfer_v,
        coupling, near_blocks,
    )
    sums = leaves * (2 * cols + rows + 3) + 2 * unroll
    y_part, z_part, n_part = pl.pallas_call(
        functools.partial(slot_kernel, rows, cols, unroll),
        out_shape=(shape(cols, 2, packs), shape(rows, packs), shape(3, packs)),
        in_specs=[SMEM] * 5 + [VMEM] * 6,
        out_specs=(VMEM,) * 3,
        scratch_shapes=[
            buf(cols * leaves, dtype=F32),
            buf(cols * leaves, dtype=F32),
            buf(rows * leaves, dtype=F32),
            buf(3 * leaves, dtype=F32),
            buf(unroll, dtype=F32),
            buf(unroll, dtype=F32),
        ],
        compiler_params=params(grant(sums * 2 * block, 2 * rows * leaves * block + (near_pairs_count * 2 + far_pairs) * 2 * block + far_pairs * wide * q * 2)),
        cost_estimate=pl.CostEstimate(flops=20_000_000_000, bytes_accessed=60_000_000, transcendentals=0),
    )(*spots, coupling_count, x_left, x_right, p_y, p_z, c_z, coupling)
    out = pl.pallas_call(
        functools.partial(down_kernel, rows, cols),
        out_shape=jax.ShapeDtypeStruct((2 * q, piece), BF),
        in_specs=[VMEM] * 12,
        out_specs=VMEM,
        scratch_shapes=[
            buf(cols - 1, 2, packs),
            buf(deep, inner - 1, packs),
            buf(deep - 1, packs),
            buf(deep - 1, packs),
            buf(2, packs),
            buf(packs),
            buf(packs, dtype=F32),
            buf(packs, dtype=F32),
            buf(packs),
            pltpu.VMEM((piece, piece), BF),
            sems(cols - 1),
            sems(deep, inner - 1),
            sems(deep - 1),
            sems(2),
        ],
        compiler_params=params(20, 1),
    )(
        y_part, z_part, n_part, sibs, order2, ubasis, vbasis, leaf_up_u, leaf_up_v,
        transfer_u, transfer_v, upper_coupling,
    )
    return out[:q], out[q:]


def solution(mesh):
    both = P(None, ("row", "col"))
    flat = P(("row", "col"))
    return jax.shard_map(
        per_device,
        mesh=mesh,
        in_specs=(both, both, flat, both, both, both, both, both, both, flat, both, both, P(), P(), P()),
        out_specs=(both, both),
        check_vma=False,
    )
```

```python
import functools

import jax
import jax.numpy as jnp
from jax import lax
from jax.experimental import pallas as pl
from jax.experimental.pallas import tpu as pltpu
from jax.sharding import PartitionSpec as P

BF = jnp.bfloat16
F32 = jnp.float32
VMEM = pl.BlockSpec(memory_space=pltpu.VMEM)
SMEM = pl.BlockSpec(memory_space=pltpu.SMEM)
NN = (((1,), (0,)), ((), ()))
NT = (((1,), (1,)), ((), ()))
UNROLL = 8


def mm(a, b, dims=NN):
    return lax.dot_general(a, b, dims, preferred_element_type=F32)


def left_mask(half, dtype):
    lane = lax.broadcasted_iota(jnp.int32, (1, 2 * half), 1)
    return (lane < half).astype(F32).astype(dtype), (lane >= half).astype(F32).astype(dtype)


def diag2(v, ml, mr):
    return jnp.concatenate([v * ml, v * mr], axis=0)


def quot(v, n):
    return lax.shift_right_logical(v, n.bit_length() - 1) if n & (n - 1) == 0 else lax.div(v, n)


def mod(v, n):
    return lax.bitwise_and(v, n - 1) if n & (n - 1) == 0 else lax.rem(v, n)


def split2(v):
    hi = v.astype(BF)
    return hi, (v - hi.astype(F32)).astype(BF)


def mm2(v, b, dims):
    hi, lo = split2(v)
    return mm(hi, b, dims) + mm(lo, b, dims)


def one_hot(order_ref, base):
    n = order_ref.shape[1]
    src = lax.broadcasted_iota(jnp.int32, (n, n), 0)
    return jnp.where(src == order_ref[...] - base, 1.0, 0.0).astype(BF)


def twin_eye(half):
    row = lax.broadcasted_iota(jnp.int32, (half, 2 * half), 0)
    lane = lax.broadcasted_iota(jnp.int32, (half, 2 * half), 1)
    return jnp.where(jnp.logical_or(lane == row, lane == row + half), 1.0, 0.0).astype(BF)


def grid_of(rows):
    inner = 1 << ((rows.bit_length() - 1) // 2)
    return rows // inner, inner


def greet(rows, cols, r, c):
    bar = pltpu.get_barrier_semaphore()
    for d in range(1, rows):
        pl.semaphore_signal(bar, inc=1, device_id={"row": lax.rem(r + d, rows)}, device_id_type=pl.DeviceIdType.MESH)
    for d in range(1, cols):
        pl.semaphore_signal(bar, inc=1, device_id={"col": lax.rem(c + d, cols)}, device_id_type=pl.DeviceIdType.MESH)
    return bar


def push(src, dst, sems, at, axis, peer):
    copy = pltpu.make_async_remote_copy(
        src_ref=src,
        dst_ref=dst,
        send_sem=sems.at[(0, *at)],
        recv_sem=sems.at[(1, *at)],
        device_id={axis: peer},
        device_id_type=pl.DeviceIdType.MESH,
    )
    copy.start()
    return copy


def chunk_at(ref, at, wide):
    return ref[:, pl.ds(pl.multiple_of(at * wide, wide), wide)]


def combine(v0, v1, fv, fu, ml, mr, isl, half):
    xp = jnp.where(isl, v0, pltpu.roll(v1, half, 1)).astype(BF)
    wp = jnp.where(isl, pltpu.roll(v0, half, 1), v1).astype(BF)
    x = mm(xp, diag2(fv, ml, mr))
    w = mm(wp, diag2(fu, ml, mr))
    return jnp.where(isl, x + pltpu.roll(x, half, 1), w + pltpu.roll(w, half, 1)).astype(BF)


def first_kernel(token_ref):
    token_ref[...] = jnp.zeros(token_ref.shape, token_ref.dtype)


def local_kernel(token_ref, far_ref, near_ref, order_ref, x_ref, w_ref, v_ref, u_ref, ev_ref, eu_ref,
                 xc_ref, xp_ref, w_out, n_ref, fi_ref, fj_ref, ni_ref, nj_ref):
    q, n = x_ref.shape
    packs = xc_ref.shape[0]
    wide = xc_ref.shape[2]
    half = wide // 2
    rows, cols = lax.axis_size("row"), lax.axis_size("col")
    my_row = lax.axis_index("row")
    base = (my_row * cols + lax.axis_index("col")) * n
    leaves = 2 * packs
    for pairs, i_ref, j_ref, near in ((far_ref, fi_ref, fj_ref, False), (near_ref, ni_ref, nj_ref, True)):
        leaf = pairs[1:2]
        group = quot(leaf, cols * leaves)
        if near:
            group = mod(group - my_row + (rows + 1), rows)
        i_ref[...] = pairs[0:1] - my_row * cols * leaves
        j_ref[...] = group * leaves + mod(leaf, leaves)
    ml, mr = left_mask(half, BF)
    isl = lax.broadcasted_iota(jnp.int32, (q, wide), 1) < half
    eye = twin_eye(half)
    hot = one_hot(order_ref, base)
    both = mm(jnp.concatenate([x_ref[...], w_ref[...]], axis=0), hot).astype(BF)
    folds = []
    for side, (b_ref, e_ref) in enumerate(((v_ref, ev_ref), (u_ref, eu_ref))):
        pts = both[side * q:(side + 1) * q]
        node = jnp.zeros((q, wide), F32)
        for m in range(packs):
            cs = slice(m * wide, (m + 1) * wide)
            pm = pts[:, cs]
            cm = mm(pm, diag2(b_ref[:, cs], ml, mr), NT).astype(BF)
            if side == 0:
                turned = diag2(pm, ml, mr)
                xc_ref[m] = mm(b_ref[:, cs], turned, NT).astype(BF)
                xp_ref[m] = mm(eye, turned, NT).astype(BF)
            else:
                w_out[0, m] = cm
                w_out[1, m] = pm
            node = node + mm(cm, diag2(e_ref[:, cs], ml, mr))
        folds.append(node + pltpu.roll(node, half, 1))
    n_ref[...] = jnp.where(isl, folds[0], folds[1]).astype(BF)


class Mail:
    def __init__(self, sem):
        self.sem = sem
        self.sent = []

    def copy(self, src, dst, recv, peer, at):
        return pltpu.make_async_remote_copy(
            src_ref=src,
            dst_ref=dst,
            send_sem=self.sem.at[at],
            recv_sem=recv,
            device_id=peer,
            device_id_type=pl.DeviceIdType.MESH,
        )

    def push(self, src, dst, recv, peer, when=None):
        args = (src, dst, recv, peer, len(self.sent))
        self.sent.append((args, when))
        guarded(when, lambda: self.copy(*args).start())

    def landed(self, dst, recv, peer):
        self.copy(dst, dst, recv, peer, 0).wait_recv()

    def close(self):
        for args, when in self.sent:
            guarded(when, lambda args=args: self.copy(*args).wait_send())


def guarded(when, act):
    if when is None:
        act()
    else:
        pl.when(when)(act)


def place(pairs, p):
    i_ref, j_ref = pairs
    return i_ref[0, 2 * p], i_ref[0, 2 * p + 1], j_ref[0, 2 * p], j_ref[0, 2 * p + 1]


def gather_kernel(rows, cols, unroll, fi_ref, fj_ref, ni_ref, nj_ref, live_ref, xc_own, xp_own, w_own, n_own, fu_ref, fv_ref, s_ref, d_ref,
                  xl, xr, pyn, pzn, pzc, sib_ref,
                  xc, xp, wa, na, nb, ql, qr, wc, wp, send_sem, x_sem, p_sem, w_sem, na_sem, nb_sem):
    packs, q, wide = xc_own.shape
    half = wide // 2
    leaves = 2 * packs
    deep, inner = grid_of(rows)
    outer = cols // 2
    dev_count = rows * cols
    first = (1 * packs) // 8
    cuts = ((0, first), (first, packs - first))
    r = lax.axis_index("row")
    c = lax.axis_index("col")
    zi = r // inner
    xi = lax.rem(r, inner)
    oi = c // 2
    ki = lax.rem(c, 2)
    live = live_ref[0]
    bar = greet(rows, cols, r, c)
    ml, mr = left_mask(half, BF)
    isl = lax.broadcasted_iota(jnp.int32, (q, wide), 1) < half
    lane = lax.broadcasted_iota(jnp.int32, (q, wide), 1)
    none = jnp.zeros((q, wide), BF)
    mail = Mail(send_sem)
    near_row = {"row": lax.rem(r + 1, rows)}
    near_col = {"col": lax.rem(c + 1, cols)}

    def row_of(z, x):
        return {"row": z * inner + x}

    def turn_x(e):
        return lax.rem(xi + e, inner)

    def xpart(row, part):
        return xc.at[row, pl.ds(*cuts[part])]

    def xown(part):
        return xc_own.at[pl.ds(*cuts[part])]

    up, down = zi < deep - 1, zi > 0
    pl.semaphore_wait(bar, rows + cols - 2)

    for e in range(1, cols):
        mail.push(n_own, na.at[c], na_sem.at[c], {"col": lax.rem(c + e, cols)})
    for kind in (1, 0):
        for e in range(1, outer):
            mail.push(w_own.at[kind], wa.at[c, kind], w_sem.at[c, kind], {"col": lax.rem(oi + e, outer) * 2 + ki})
        mail.push(w_own.at[kind], wa.at[c, kind], w_sem.at[c, kind], {"col": oi * 2 + 1 - ki})
    for e in range(1, inner):
        mail.push(xown(0), xpart(r, 0), x_sem.at[r, 0], row_of(zi, turn_x(e)))
    for part in (1, 0):
        mail.push(xown(part), xpart(r, part), x_sem.at[r, part], row_of(zi + 1, xi), up)
        mail.push(xown(part), xpart(r, part), x_sem.at[r, part], row_of(zi - 1, xi), down)
    if inner == 2:
        mail.push(xp_own, xp.at[2 * xi], p_sem.at[2 * xi], row_of(zi, 1 - xi))
    else:
        mail.push(xp_own, xp.at[0], p_sem.at[0], {"row": lax.rem(r + 1, rows)})
        mail.push(xp_own, xp.at[2], p_sem.at[2], {"row": lax.rem(r + rows - 1, rows)})
    for e in range(1, inner):
        mail.push(xown(1), xpart(r, 1), x_sem.at[r, 1], row_of(zi, turn_x(e)))

    def split(v, left, right, at):
        t = jnp.concatenate([v[:, half:], v[:, :half]], axis=1)
        left[at] = jnp.where(isl, v, none)
        left[at + 1] = jnp.where(isl, t, none)
        right[at] = jnp.where(isl, none, t)
        right[at + 1] = jnp.where(isl, none, v)

    def widen(v, table, at):
        t = jnp.concatenate([v[:, half:], v[:, :half]], axis=1)
        table[at] = jnp.where(isl, v, t)
        table[at + 1] = jnp.where(isl, t, v)

    def each_pack(act):
        for m in range(packs):
            act(m)

    def own_fill(m):
        split(xc_own[m], xl, xr, 2 * (r * packs + m))
        split(xp_own[m], ql, qr, 2 * (packs + m))
        widen(w_own[0, m], wc, 2 * (c * packs + m))
        widen(w_own[1, m], wp, 2 * (c * packs + m))

    each_pack(own_fill)

    me = r * cols + c
    for e in range(1, cols):
        o = lax.rem(c + e, cols)
        mail.landed(na.at[o], na_sem.at[o], near_col)
    na[c] = n_own[...]
    vals = [na[i].astype(F32) for i in range(cols)]
    level = 0
    while len(vals) > 1:
        own = c >> level
        sib_ref[level] = pick(vals, own + 1 - 2 * lax.rem(own, 2)).astype(BF)
        off = dev_count - (dev_count >> level)
        count = len(vals) // 2
        vals = [
            combine(vals[2 * i], vals[2 * i + 1], chunk_at(fv_ref, off + r * count + i, wide),
                    chunk_at(fu_ref, off + r * count + i, wide), ml, mr, isl, half).astype(F32)
            for i in range(count)
        ]
        level += 1
    base_level = level
    top = [vals[0]]

    def ask(t):
        nb[2 * t] = top[0].astype(BF)
        mail.push(nb.at[2 * t], nb.at[2 * t + 1], nb_sem.at[t], {"row": r + (1 << t) * (1 - 2 * lax.rem(r >> t, 2))})

    def answer(t):
        mail.landed(nb.at[2 * t + 1], nb_sem.at[t], near_row)
        lev = base_level + t
        sib_ref[lev] = nb[2 * t + 1]
        if dev_count >> (lev + 1) > 1:
            other = nb[2 * t + 1].astype(F32)
            even = lax.rem(r >> t, 2) == 0
            lo = jnp.where(even, top[0], other)
            hi = jnp.where(even, other, top[0])
            at = dev_count - (dev_count >> lev) + ((me >> lev) >> 1)
            top[0] = combine(lo, hi, chunk_at(fv_ref, at, wide), chunk_at(fu_ref, at, wide), ml, mr, isl, half).astype(F32)
            ask(t + 1)

    row_levels = rows.bit_length() - 1
    ask(0)

    def relay_across():
        for e in range(1, inner):
            o = zi * inner + turn_x(e)
            mail.landed(xpart(o, 0), x_sem.at[o, 0], near_row)
            mail.push(xpart(o, 0), xpart(o, 0), x_sem.at[o, 0], row_of(zi + 1, xi), up)
            mail.push(xpart(o, 0), xpart(o, 0), x_sem.at[o, 0], row_of(zi - 1, xi), down)

    def relay_along(d, e, part):
        for back in (True, False):
            have = zi >= d if back else zi + d < deep
            oz = zi - d if back else zi + d
            o = oz * inner + turn_x(e)
            guarded(have, lambda o=o: mail.landed(xpart(o, part), x_sem.at[o, part], near_row))
            if d < deep - 1:
                onward = jnp.logical_and(have, up if back else down)
                mail.push(xpart(o, part), xpart(o, part), x_sem.at[o, part], row_of(zi + 1 if back else zi - 1, xi), onward)
            if part == 1:
                for f in range(1, inner):
                    mail.push(xpart(o, 1), xpart(o, 1), x_sem.at[o, 1], row_of(zi, turn_x(f)), have)

    def relay_points():
        if inner == 2:
            got = 2 * (1 - xi)
            mail.landed(xp.at[got], p_sem.at[got], near_row)
            to = lax.rem(zi + deep + 1 - 2 * xi, deep)
            mail.push(xp.at[got], xp.at[2 * xi], p_sem.at[2 * xi], row_of(to, xi))

    def relay_w(kind):
        for e in range(1, outer):
            o = lax.rem(oi + e, outer) * 2 + ki
            mail.landed(wa.at[o, kind], w_sem.at[o, kind], near_col)
            mail.push(wa.at[o, kind], wa.at[o, kind], w_sem.at[o, kind], {"col": oi * 2 + 1 - ki})

    def fill_w(kind, table):
        for e in range(outer):
            o = lax.rem(oi + e, outer) * 2 + 1 - ki
            mail.landed(wa.at[o, kind], w_sem.at[o, kind], near_col)
        for e in range(1, cols):
            o = lax.rem(c + e, cols)
            each_pack(lambda m, o=o: widen(wa[o, kind, m], table, 2 * (o * packs + m)))

    def fill_p():
        if inner == 2:
            mail.landed(xp.at[2 * xi], p_sem.at[2 * xi], near_row)
        else:
            mail.landed(xp.at[0], p_sem.at[0], near_row)
            mail.landed(xp.at[2], p_sem.at[2], near_row)
        for k in (0, 2):
            each_pack(lambda m, k=k: split(xp[k, m], ql, qr, 2 * (k * packs + m)))

    def products(pairs, mat, near, side, tables, out, piece, pieces):
        total = out.shape[0] // unroll
        def step(g, carry):
            for k in range(unroll):
                p = g * unroll + k
                i0, i1, j0, j1 = place(pairs, p)
                blk = mat[:, pl.ds(pl.multiple_of(p * wide, wide), wide)]
                if side == "z":
                    if not near:
                        reach = jnp.where(2 * p + 1 < live, wide, jnp.where(2 * p < live, half, 0))
                        blk = jnp.where(lane < reach, blk, none)
                    pair = jnp.concatenate([jnp.where(isl, blk, none), jnp.where(isl, none, blk)], axis=0)
                    out[p] = mm(jnp.where(isl, tables[i0], tables[i1]), pair)
                else:
                    out[p] = mm(blk, jnp.concatenate([tables[0][j0], tables[1][j1]], axis=0))
            return carry
        lax.fori_loop(piece * total // pieces, (piece + 1) * total // pieces, step, 0)

    def near_z(k, n):
        products((ni_ref, nj_ref), d_ref, True, "z", wp, pzn, k, n)

    def far_z(k, n):
        products((fi_ref, fj_ref), s_ref, False, "z", wc, pzc, k, n)

    def near_y(k, n):
        products((ni_ref, nj_ref), d_ref, True, "y", (ql, qr), pyn, k, n)

    def fill_rows(e):
        def step(dz, carry):
            o = lax.rem(zi + dz, deep) * inner + turn_x(e)
            for m in range(packs):
                split(xc[o, m], xl, xr, 2 * (o * packs + m))
            return carry
        lax.fori_loop(1 if e == 0 else 0, deep, step, 0)

    relay_across()
    relay_along(1, 0, 1)
    relay_along(1, 0, 0)
    for e in range(1, inner):
        relay_along(1, e, 0)
    relay_w(1)
    answer(0)
    if deep <= 2:
        relay_points()
        relay_w(0)
    for d in range(2, deep):
        relay_along(d, 0, 1)
        relay_along(d, 0, 0)
        if d == 2:
            relay_points()
            relay_w(0)
        for e in range(1, inner):
            relay_along(d, e, 0)
        if d == 2:
            if row_levels > 1:
                answer(1)
            fill_w(1, wp)
            near_z(0, 1)
            fill_w(0, wc)
            far_z(0, 2)
    if deep <= 2:
        fill_w(1, wp)
        near_z(0, 1)
        fill_w(0, wc)
        far_z(0, 2)
    far_z(1, 2)
    fill_rows(0)
    fill_p()
    near_y(0, 1)
    for t in range(2 if deep > 2 else 1, row_levels):
        answer(t)
    for e in range(1, inner):
        for dz in range(deep):
            o = lax.rem(zi + dz, deep) * inner + turn_x(e)
            mail.landed(xpart(o, 1), x_sem.at[o, 1], near_row)
        fill_rows(e)
    mail.close()


def pick(vals, at):
    out = vals[0]
    for i in range(1, len(vals)):
        out = jnp.where(at == i, vals[i], out)
    return out


def grant(own, operands):
    mib = 1024 * 1024
    return own // mib + 5 if own + operands < 40 * mib else min(62, (own + operands) // mib + 6)


def slot_kernel(rows, cols, unroll, fi_ref, fj_ref, ni_ref, nj_ref, live_ref, xl, xr, pyn, pzn, pzc, s_ref, y_ref, z_ref, n_ref,
                yc, yn, zc, zn, y0, y1):
    _, q, wide = xl.shape
    half = wide // 2
    packs = z_ref.shape[1]
    leaves = 2 * packs
    live = live_ref[0]
    isl = lax.broadcasted_iota(jnp.int32, (q, wide), 1) < half
    lane = lax.broadcasted_iota(jnp.int32, (q, wide), 1)
    none = jnp.zeros((q, wide), BF)
    blank = jnp.zeros((q, wide), F32)

    def clear(acc):
        group = 8
        def step(i, carry):
            for k in range(group):
                acc[i * group + k] = blank
            return carry
        lax.fori_loop(0, acc.shape[0] // group, step, 0)

    for acc in (yc, yn, zc, zn):
        clear(acc)

    def settle(pairs, p, yv, zv, ya, za):
        i0, i1, j0, j1 = place(pairs, p)
        a = ya[i0, :, :half] + yv[:, :half]
        b = ya[i1, :, half:] + yv[:, half:]
        c = za[j0, :, :half] + zv[:, :half]
        d = za[j1, :, half:] + zv[:, half:]
        ya[i0, :, :half] = a
        ya[i1, :, half:] = b
        za[j0, :, :half] = c
        za[j1, :, half:] = d

    def near_step(g, carry):
        for k in range(unroll):
            p = g * unroll + k
            settle((ni_ref, nj_ref), p, pyn[p], pzn[p], yn, zn)
        return carry

    lax.fori_loop(0, ni_ref.shape[1] // (2 * unroll), near_step, 0)

    def far(g, buf):
        for k in range(unroll):
            p = g * unroll + k
            settle((fi_ref, fj_ref), p, buf[k], pzc[p], yc, zc)

    def multiply(g, buf):
        for k in range(unroll):
            p = g * unroll + k
            j0, j1 = fj_ref[0, 2 * p], fj_ref[0, 2 * p + 1]
            blk = s_ref[:, pl.ds(pl.multiple_of(p * wide, wide), wide)]
            reach = jnp.where(2 * p + 1 < live, wide, jnp.where(2 * p < live, half, 0))
            blk = jnp.where(lane < reach, blk, none)
            top = xl[j0]
            bot = xr[j1]
            pair = jnp.concatenate([top, bot], axis=0)
            buf[k] = mm(blk, pair)

    steps = quot(live + 4 * unroll - 1, 4 * unroll)
    multiply(0, y0)
    def step(g, carry):
        multiply(2 * g + 1, y1)
        far(2 * g, y0)
        multiply(2 * g + 2, y0)
        far(2 * g + 1, y1)
        return carry
    lax.fori_loop(0, steps - 1, step, 0)
    multiply(2 * steps - 1, y1)
    far(2 * steps - 2, y0)
    far(2 * steps - 1, y1)

    def fold(acc, at):
        a, b = acc[at], acc[at + 1]
        return (jnp.where(isl, a, b) + pltpu.roll(jnp.where(isl, b, a), half, 1)).astype(BF)

    def out_y(i, carry):
        for kind, acc in enumerate((yc, yn)):
            for m in range(packs):
                y_ref[i, kind, m] = fold(acc, 2 * (i * packs + m))
        return carry

    def out_z(i, carry):
        for m in range(packs):
            z_ref[i, m] = fold(zc, 2 * (i * packs + m))
        return carry

    def out_n(i, carry):
        for m in range(packs):
            n_ref[i, m] = fold(zn, 2 * (i * packs + m))
        return carry

    lax.fori_loop(0, cols, out_y, 0)
    lax.fori_loop(0, rows, out_z, 0)
    lax.fori_loop(0, 3, out_n, 0)


def down_kernel(rows, cols, y_ref, z_ref, n_ref, sib_ref, order_ref, u_ref, v_ref, eu_ref, ev_ref, fu_ref, fv_ref,
                s_ref, o_ref, y_in, z1_in, z1_out, z2_in, zn_in, zn_out, ahead_y, ahead_z, u_turn, hot_turn,
                y_sem, z1_sem, z2_sem, n_sem):
    _, packs, q, wide = z_ref.shape
    half = wide // 2
    deep, inner = grid_of(rows)
    dev_count = rows * cols
    r = lax.axis_index("row")
    c = lax.axis_index("col")
    me = r * cols + c
    zi = r // inner
    xi = lax.rem(r, inner)
    bar = greet(rows, cols, r, c)
    ml, mr = left_mask(half, BF)
    isl = lax.broadcasted_iota(jnp.int32, (q, wide), 1) < half
    eye = twin_eye(half)
    pl.semaphore_wait(bar, rows + cols - 2)
    folded = inner == 2
    if folded:
        to = lax.rem(zi + deep - 1 + 2 * xi, deep) * inner + xi
        near = [push(n_ref.at[2 * xi], zn_in.at[0], n_sem, (0,), "row", to)]
    else:
        near = [
            push(n_ref.at[0], zn_in.at[0], n_sem, (0,), "row", lax.rem(r + rows - 1, rows)),
            push(n_ref.at[2], zn_in.at[1], n_sem, (1,), "row", lax.rem(r + 1, rows)),
        ]
    first = {}
    for d in list(range(1, deep)) + [0]:
        to = lax.rem(zi + d, deep) * inner
        first[d] = []
        for e in range(1, inner):
            peer = lax.rem(xi + e, inner)
            first[d].append(
                push(z_ref.at[to + peer], z1_in.at[d, e - 1], z1_sem, (d, e - 1), "row", zi * inner + peer)
            )
    y_copies = []
    for d in range(1, cols):
        peer = lax.rem(c + d, cols)
        y_copies.append(push(y_ref.at[peer], y_in.at[d - 1], y_sem, (d - 1,), "col", peer))

    levels = dev_count.bit_length() - 1
    lane_half = (lax.broadcasted_iota(jnp.int32, (q, wide), 1) >= half).astype(jnp.int32)

    def turned(v, chunk, side):
        return mm2(jnp.where(lane_half == side, v, 0.0), jnp.concatenate([chunk, chunk], axis=0), NT)

    y_down = z_down = None
    for level in range(levels - 1, -1, -1):
        own = me >> level
        side = lax.rem(own, 2)
        sib = sib_ref[level].astype(F32)
        rolled = pltpu.roll(sib, half, 1)
        xs = jnp.where(isl, sib, rolled)
        ws = jnp.where(isl, rolled, 0.0).astype(BF)
        at = dev_count - (dev_count >> level) + own // 2
        cup = chunk_at(s_ref, at, wide)
        dup = jnp.concatenate([cup, cup], axis=0)
        y_term = mm(jnp.where(lane_half == side, xs, 0.0).astype(BF), dup, NT)
        z_raw = jnp.where(lane_half == 1 - side, mm(ws, dup), 0.0)
        z_term = z_raw + pltpu.roll(z_raw, half, 1)
        if level < levels - 1:
            y_term = y_term + turned(y_down, chunk_at(fu_ref, at, wide), side)
            z_term = z_term + turned(z_down, chunk_at(fv_ref, at, wide), side)
        y_down, z_down = y_term, z_term

    second = []

    def pass_on(d):
        for copy in first[d]:
            copy.wait_recv()
        to = lax.rem(zi + d, deep) * inner + xi
        for m in range(packs):
            total = z_ref[to, m].astype(F32)
            for e in range(inner - 1):
                total = total + z1_in[d, e, m].astype(F32)
            z1_out[d - 1, m] = total.astype(BF)
        second.append(push(z1_out.at[d - 1], z2_in.at[d - 1], z2_sem, (d - 1,), "row", to))

    def pass_near():
        if folded:
            near[0].wait_recv()
            for m in range(packs):
                zn_out[m] = (zn_in[0, m].astype(F32) + n_ref[2 * (1 - xi), m].astype(F32)).astype(BF)
            near.append(push(zn_out, zn_in.at[1], n_sem, (1,), "row", zi * inner + 1 - xi))

    def columns(m):
        return slice(m * wide, (m + 1) * wide)

    if deep > 1:
        pass_on(1)
    pass_near()
    hi, lo = split2(y_down)
    hi, lo = diag2(hi, ml, mr), diag2(lo, ml, mr)
    for m in range(packs):
        e = eu_ref[:, columns(m)]
        ahead_y[m] = mm(e, hi, NT) + mm(e, lo, NT)
        ahead_z[m] = mm2(z_down, diag2(ev_ref[:, columns(m)], ml, mr), NT)
        u_turn[m] = mm(eye, diag2(u_ref[:, columns(m)], ml, mr), NT).astype(BF)
    if deep > 2:
        pass_on(2)
    hot_turn[...] = jnp.transpose(one_hot(order_ref, me * order_ref.shape[1]))
    for d in range(3, deep):
        pass_on(d)

    for copy in y_copies:
        copy.wait_recv()
    parts = []
    for m in range(packs):
        coef, raw = y_ref[c, 0, m].astype(F32), y_ref[c, 1, m].astype(F32)
        for d in range(cols - 1):
            coef = coef + y_in[d, 0, m].astype(F32)
            raw = raw + y_in[d, 1, m].astype(F32)
        leaf = (coef + ahead_y[m]).astype(BF)
        pts = (mm(u_turn[m], diag2(leaf, ml, mr)) + raw).astype(BF)
        parts.append(mm(eye, diag2(pts, ml, mr), NT).astype(BF))
    o_ref[:q] = mm(jnp.concatenate(parts, axis=1), hot_turn[...]).astype(BF)

    for copy in first[0] + second + near[1 if folded else 0:]:
        copy.wait_recv()
    parts = []
    for m in range(packs):
        coef, raw = z_ref[r, m].astype(F32), n_ref[1, m].astype(F32)
        for e in range(inner - 1):
            coef = coef + z1_in[0, e, m].astype(F32)
        for d in range(deep - 1):
            coef = coef + z2_in[d, m].astype(F32)
        for k in ((1,) if folded else (0, 1)):
            raw = raw + zn_in[k, m].astype(F32)
        leaf = (coef + ahead_z[m]).astype(BF)
        parts.append((mm(leaf, diag2(v_ref[:, columns(m)], ml, mr)) + raw).astype(BF))
    o_ref[q:] = mm(jnp.concatenate(parts, axis=1), hot_turn[...]).astype(BF)
    for copies in (*first.values(), second, near, y_copies):
        for copy in copies:
            copy.wait_send()


def per_device(
    x_vectors,
    w_vectors,
    order,
    ubasis,
    vbasis,
    leaf_up_u,
    leaf_up_v,
    coupling,
    coupling_pairs,
    coupling_count,
    near_blocks,
    near_pairs,
    transfer_u,
    transfer_v,
    upper_coupling,
):
    q, piece = x_vectors.shape
    rank = ubasis.shape[0]
    leaves = leaf_up_u.shape[1] // rank
    packs = leaves // 2
    wide = 2 * rank
    rows = lax.axis_size("row")
    cols = lax.axis_size("col")
    deep, inner = grid_of(rows)
    order2 = order.reshape(1, piece)

    def shape(*lead):
        return jax.ShapeDtypeStruct((*lead, q, wide), BF)

    def wide_shape(*lead):
        return jax.ShapeDtypeStruct((*lead, q, wide), F32)

    def buf(*lead, dtype=BF):
        return pltpu.VMEM((*lead, q, wide), dtype)

    def sems(*lead):
        return pltpu.SemaphoreType.DMA((2, *lead))

    def params(mib, cid=None):
        limit = mib * 1024 * 1024
        if cid is None:
            return pltpu.CompilerParams(vmem_limit_bytes=limit)
        return pltpu.CompilerParams(vmem_limit_bytes=limit, collective_id=cid, has_side_effects=True)

    token = pl.pallas_call(
        first_kernel,
        out_shape=jax.ShapeDtypeStruct((1, wide), F32),
        out_specs=VMEM,
        compiler_params=params(1),
        cost_estimate=pl.CostEstimate(flops=2_000_000_000, bytes_accessed=6_000_000, transcendentals=0),
    )()
    loaded = (token, coupling_pairs, near_pairs, order2, x_vectors, w_vectors, vbasis, ubasis, leaf_up_v, leaf_up_u)
    own_x, own_p, own_w, own_n, *spots = pl.pallas_call(
        local_kernel,
        out_shape=(
            shape(packs), shape(packs), shape(2, packs), shape(),
            *(jax.ShapeDtypeStruct((1, v.shape[1]), jnp.int32) for v in (coupling_pairs, coupling_pairs, near_pairs, near_pairs)),
        ),
        in_specs=[VMEM] * 10,
        out_specs=(VMEM,) * 8,
        compiler_params=params(12),
        cost_estimate=pl.CostEstimate(flops=8_000_000, bytes_accessed=20_000, transcendentals=0),
    )(*loaded)
    unroll = UNROLL
    far_pairs = coupling_pairs.shape[1] // 2
    near_pairs_count = near_pairs.shape[1] // 2
    levels = (rows * cols).bit_length() - 1
    row_levels = rows.bit_length() - 1
    tables = 2 * leaves * (3 + cols)
    raw = packs * (rows + 3 + 2 * cols)
    block = q * wide * 2
    x_left, x_right, p_y, p_z, c_z, sibs = pl.pallas_call(
        functools.partial(gather_kernel, rows, cols, 32),
        out_shape=(
            shape(rows * leaves), shape(rows * leaves), wide_shape(near_pairs_count), wide_shape(near_pairs_count),
            wide_shape(far_pairs), shape(levels),
        ),
        in_specs=[SMEM] * 5 + [VMEM] * 8,
        out_specs=(VMEM,) * 6,
        scratch_shapes=[
            buf(rows, packs),
            buf(3, packs),
            buf(cols, 2, packs),
            buf(cols),
            buf(2 * row_levels),
            buf(3 * leaves),
            buf(3 * leaves),
            buf(cols * leaves),
            buf(cols * leaves),
            pltpu.SemaphoreType.DMA((128,)),
            pltpu.SemaphoreType.DMA((rows, 2)),
            pltpu.SemaphoreType.DMA((3,)),
            pltpu.SemaphoreType.DMA((cols, 2)),
            pltpu.SemaphoreType.DMA((cols,)),
            pltpu.SemaphoreType.DMA((row_levels,)),
        ],
        compiler_params=params(6 + (tables + raw) * block // 1024**2, 0),
        cost_estimate=pl.CostEstimate(flops=20_000_000_000, bytes_accessed=60_000_000, transcendentals=0),
    )(
        *spots, coupling_count, own_x, own_p, own_w, own_n, transfer_u, transfer_v,
        coupling, near_blocks,
    )
    sums = leaves * (2 * cols + rows + 3) + 2 * unroll
    y_part, z_part, n_part = pl.pallas_call(
        functools.partial(slot_kernel, rows, cols, unroll),
        out_shape=(shape(cols, 2, packs), shape(rows, packs), shape(3, packs)),
        in_specs=[SMEM] * 5 + [VMEM] * 6,
        out_specs=(VMEM,) * 3,
        scratch_shapes=[
            buf(cols * leaves, dtype=F32),
            buf(cols * leaves, dtype=F32),
            buf(rows * leaves, dtype=F32),
            buf(3 * leaves, dtype=F32),
            buf(unroll, dtype=F32),
            buf(unroll, dtype=F32),
        ],
        compiler_params=params(grant(sums * 2 * block, 2 * rows * leaves * block + (near_pairs_count * 2 + far_pairs) * 2 * block + far_pairs * wide * q * 2)),
        cost_estimate=pl.CostEstimate(flops=20_000_000_000, bytes_accessed=60_000_000, transcendentals=0),
    )(*spots, coupling_count, x_left, x_right, p_y, p_z, c_z, coupling)
    out = pl.pallas_call(
        functools.partial(down_kernel, rows, cols),
        out_shape=jax.ShapeDtypeStruct((2 * q, piece), BF),
        in_specs=[VMEM] * 12,
        out_specs=VMEM,
        scratch_shapes=[
            buf(cols - 1, 2, packs),
            buf(deep, inner - 1, packs),
            buf(deep - 1, packs),
            buf(deep - 1, packs),
            buf(2, packs),
            buf(packs),
            buf(packs, dtype=F32),
            buf(packs, dtype=F32),
            buf(packs),
            pltpu.VMEM((piece, piece), BF),
            sems(cols - 1),
            sems(deep, inner - 1),
            sems(deep - 1),
            sems(2),
        ],
        compiler_params=params(20, 1),
    )(
        y_part, z_part, n_part, sibs, order2, ubasis, vbasis, leaf_up_u, leaf_up_v,
        transfer_u, transfer_v, upper_coupling,
    )
    return out[:q], out[q:]


def solution(mesh):
    both = P(None, ("row", "col"))
    flat = P(("row", "col"))
    return jax.shard_map(
        per_device,
        mesh=mesh,
        in_specs=(both, both, flat, both, both, both, both, both, both, flat, both, both, P(), P(), P()),
        out_specs=(both, both),
        check_vma=False,
    )
```

```python
import functools

import jax
import jax.numpy as jnp
from jax import lax
from jax.experimental import pallas as pl
from jax.experimental.pallas import tpu as pltpu
from jax.sharding import PartitionSpec as P

BF = jnp.bfloat16
F32 = jnp.float32
VMEM = pl.BlockSpec(memory_space=pltpu.VMEM)
SMEM = pl.BlockSpec(memory_space=pltpu.SMEM)
NN = (((1,), (0,)), ((), ()))
NT = (((1,), (1,)), ((), ()))
UNROLL = 16


def mm(a, b, dims=NN):
    return lax.dot_general(a, b, dims, preferred_element_type=F32)


def left_mask(half, dtype):
    lane = lax.broadcasted_iota(jnp.int32, (1, 2 * half), 1)
    return (lane < half).astype(F32).astype(dtype), (lane >= half).astype(F32).astype(dtype)


def diag2(v, ml, mr):
    return jnp.concatenate([v * ml, v * mr], axis=0)


def quot(v, n):
    return lax.shift_right_logical(v, n.bit_length() - 1) if n & (n - 1) == 0 else lax.div(v, n)


def mod(v, n):
    return lax.bitwise_and(v, n - 1) if n & (n - 1) == 0 else lax.rem(v, n)


def split2(v):
    hi = v.astype(BF)
    return hi, (v - hi.astype(F32)).astype(BF)


def mm2(v, b, dims):
    hi, lo = split2(v)
    return mm(hi, b, dims) + mm(lo, b, dims)


def one_hot(order_ref, base):
    n = order_ref.shape[1]
    src = lax.broadcasted_iota(jnp.int32, (n, n), 0)
    return jnp.where(src == order_ref[...] - base, 1.0, 0.0).astype(BF)


def twin_eye(half):
    row = lax.broadcasted_iota(jnp.int32, (half, 2 * half), 0)
    lane = lax.broadcasted_iota(jnp.int32, (half, 2 * half), 1)
    return jnp.where(jnp.logical_or(lane == row, lane == row + half), 1.0, 0.0).astype(BF)


def grid_of(rows):
    inner = 1 << ((rows.bit_length() - 1) // 2)
    return rows // inner, inner


def greet(rows, cols, r, c):
    bar = pltpu.get_barrier_semaphore()
    for d in range(1, rows):
        pl.semaphore_signal(bar, inc=1, device_id={"row": lax.rem(r + d, rows)}, device_id_type=pl.DeviceIdType.MESH)
    for d in range(1, cols):
        pl.semaphore_signal(bar, inc=1, device_id={"col": lax.rem(c + d, cols)}, device_id_type=pl.DeviceIdType.MESH)
    return bar


def push(src, dst, sems, at, axis, peer):
    copy = pltpu.make_async_remote_copy(
        src_ref=src,
        dst_ref=dst,
        send_sem=sems.at[(0, *at)],
        recv_sem=sems.at[(1, *at)],
        device_id={axis: peer},
        device_id_type=pl.DeviceIdType.MESH,
    )
    copy.start()
    return copy


def chunk_at(ref, at, wide):
    return ref[:, pl.ds(pl.multiple_of(at * wide, wide), wide)]


def combine(v0, v1, fv, fu, ml, mr, isl, half):
    xp = jnp.where(isl, v0, pltpu.roll(v1, half, 1)).astype(BF)
    wp = jnp.where(isl, pltpu.roll(v0, half, 1), v1).astype(BF)
    x = mm(xp, diag2(fv, ml, mr))
    w = mm(wp, diag2(fu, ml, mr))
    return jnp.where(isl, x + pltpu.roll(x, half, 1), w + pltpu.roll(w, half, 1)).astype(BF)


def first_kernel(token_ref):
    token_ref[...] = jnp.zeros(token_ref.shape, token_ref.dtype)


def local_kernel(token_ref, far_ref, near_ref, order_ref, x_ref, w_ref, v_ref, u_ref, ev_ref, eu_ref,
                 xc_ref, xp_ref, w_out, n_ref, fi_ref, fj_ref, ni_ref, nj_ref):
    q, n = x_ref.shape
    packs = xc_ref.shape[0]
    wide = xc_ref.shape[2]
    half = wide // 2
    rows, cols = lax.axis_size("row"), lax.axis_size("col")
    my_row = lax.axis_index("row")
    base = (my_row * cols + lax.axis_index("col")) * n
    leaves = 2 * packs
    for pairs, i_ref, j_ref, near in ((far_ref, fi_ref, fj_ref, False), (near_ref, ni_ref, nj_ref, True)):
        leaf = pairs[1:2]
        group = quot(leaf, cols * leaves)
        if near:
            group = mod(group - my_row + (rows + 1), rows)
        i_ref[...] = pairs[0:1] - my_row * cols * leaves
        j_ref[...] = group * leaves + mod(leaf, leaves)
    ml, mr = left_mask(half, BF)
    isl = lax.broadcasted_iota(jnp.int32, (q, wide), 1) < half
    eye = twin_eye(half)
    hot = one_hot(order_ref, base)
    both = mm(jnp.concatenate([x_ref[...], w_ref[...]], axis=0), hot).astype(BF)
    folds = []
    for side, (b_ref, e_ref) in enumerate(((v_ref, ev_ref), (u_ref, eu_ref))):
        pts = both[side * q:(side + 1) * q]
        node = jnp.zeros((q, wide), F32)
        for m in range(packs):
            cs = slice(m * wide, (m + 1) * wide)
            pm = pts[:, cs]
            cm = mm(pm, diag2(b_ref[:, cs], ml, mr), NT).astype(BF)
            if side == 0:
                turned = diag2(pm, ml, mr)
                xc_ref[m] = mm(b_ref[:, cs], turned, NT).astype(BF)
                xp_ref[m] = mm(eye, turned, NT).astype(BF)
            else:
                w_out[0, m] = cm
                w_out[1, m] = pm
            node = node + mm(cm, diag2(e_ref[:, cs], ml, mr))
        folds.append(node + pltpu.roll(node, half, 1))
    n_ref[...] = jnp.where(isl, folds[0], folds[1]).astype(BF)


class Mail:
    def __init__(self, sem):
        self.sem = sem
        self.sent = []

    def copy(self, src, dst, recv, peer, at):
        return pltpu.make_async_remote_copy(
            src_ref=src,
            dst_ref=dst,
            send_sem=self.sem.at[at],
            recv_sem=recv,
            device_id=peer,
            device_id_type=pl.DeviceIdType.MESH,
        )

    def push(self, src, dst, recv, peer, when=None):
        args = (src, dst, recv, peer, len(self.sent))
        self.sent.append((args, when))
        guarded(when, lambda: self.copy(*args).start())

    def landed(self, dst, recv, peer):
        self.copy(dst, dst, recv, peer, 0).wait_recv()

    def close(self):
        for args, when in self.sent:
            guarded(when, lambda args=args: self.copy(*args).wait_send())


def guarded(when, act):
    if when is None:
        act()
    else:
        pl.when(when)(act)


def place(pairs, p):
    i_ref, j_ref = pairs
    return i_ref[0, 2 * p], i_ref[0, 2 * p + 1], j_ref[0, 2 * p], j_ref[0, 2 * p + 1]


def gather_kernel(rows, cols, unroll, fi_ref, fj_ref, ni_ref, nj_ref, live_ref, xc_own, xp_own, w_own, n_own, fu_ref, fv_ref, s_ref, d_ref,
                  xl, xr, pyn, pzn, pzc, sib_ref,
                  xc, xp, wa, na, nb, ql, qr, wc, wp, send_sem, x_sem, p_sem, w_sem, na_sem, nb_sem):
    packs, q, wide = xc_own.shape
    half = wide // 2
    leaves = 2 * packs
    deep, inner = grid_of(rows)
    outer = cols // 2
    dev_count = rows * cols
    first = (1 * packs) // 8
    cuts = ((0, first), (first, packs - first))
    r = lax.axis_index("row")
    c = lax.axis_index("col")
    zi = r // inner
    xi = lax.rem(r, inner)
    oi = c // 2
    ki = lax.rem(c, 2)
    live = live_ref[0]
    bar = greet(rows, cols, r, c)
    ml, mr = left_mask(half, BF)
    isl = lax.broadcasted_iota(jnp.int32, (q, wide), 1) < half
    lane = lax.broadcasted_iota(jnp.int32, (q, wide), 1)
    none = jnp.zeros((q, wide), BF)
    mail = Mail(send_sem)
    near_row = {"row": lax.rem(r + 1, rows)}
    near_col = {"col": lax.rem(c + 1, cols)}

    def row_of(z, x):
        return {"row": z * inner + x}

    def turn_x(e):
        return lax.rem(xi + e, inner)

    def xpart(row, part):
        return xc.at[row, pl.ds(*cuts[part])]

    def xown(part):
        return xc_own.at[pl.ds(*cuts[part])]

    up, down = zi < deep - 1, zi > 0
    pl.semaphore_wait(bar, rows + cols - 2)

    for e in range(1, cols):
        mail.push(n_own, na.at[c], na_sem.at[c], {"col": lax.rem(c + e, cols)})
    for kind in (1, 0):
        for e in range(1, outer):
            mail.push(w_own.at[kind], wa.at[c, kind], w_sem.at[c, kind], {"col": lax.rem(oi + e, outer) * 2 + ki})
        mail.push(w_own.at[kind], wa.at[c, kind], w_sem.at[c, kind], {"col": oi * 2 + 1 - ki})
    for e in range(1, inner):
        mail.push(xown(0), xpart(r, 0), x_sem.at[r, 0], row_of(zi, turn_x(e)))
    for part in (1, 0):
        mail.push(xown(part), xpart(r, part), x_sem.at[r, part], row_of(zi + 1, xi), up)
        mail.push(xown(part), xpart(r, part), x_sem.at[r, part], row_of(zi - 1, xi), down)
    if inner == 2:
        mail.push(xp_own, xp.at[2 * xi], p_sem.at[2 * xi], row_of(zi, 1 - xi))
    else:
        mail.push(xp_own, xp.at[0], p_sem.at[0], {"row": lax.rem(r + 1, rows)})
        mail.push(xp_own, xp.at[2], p_sem.at[2], {"row": lax.rem(r + rows - 1, rows)})
    for e in range(1, inner):
        mail.push(xown(1), xpart(r, 1), x_sem.at[r, 1], row_of(zi, turn_x(e)))

    def split(v, left, right, at):
        t = jnp.concatenate([v[:, half:], v[:, :half]], axis=1)
        left[at] = jnp.where(isl, v, none)
        left[at + 1] = jnp.where(isl, t, none)
        right[at] = jnp.where(isl, none, t)
        right[at + 1] = jnp.where(isl, none, v)

    def widen(v, table, at):
        t = jnp.concatenate([v[:, half:], v[:, :half]], axis=1)
        table[at] = jnp.where(isl, v, t)
        table[at + 1] = jnp.where(isl, t, v)

    def each_pack(act):
        for m in range(packs):
            act(m)

    def own_fill(m):
        split(xc_own[m], xl, xr, 2 * (r * packs + m))
        split(xp_own[m], ql, qr, 2 * (packs + m))
        widen(w_own[0, m], wc, 2 * (c * packs + m))
        widen(w_own[1, m], wp, 2 * (c * packs + m))

    each_pack(own_fill)

    me = r * cols + c
    for e in range(1, cols):
        o = lax.rem(c + e, cols)
        mail.landed(na.at[o], na_sem.at[o], near_col)
    na[c] = n_own[...]
    vals = [na[i].astype(F32) for i in range(cols)]
    level = 0
    while len(vals) > 1:
        own = c >> level
        sib_ref[level] = pick(vals, own + 1 - 2 * lax.rem(own, 2)).astype(BF)
        off = dev_count - (dev_count >> level)
        count = len(vals) // 2
        vals = [
            combine(vals[2 * i], vals[2 * i + 1], chunk_at(fv_ref, off + r * count + i, wide),
                    chunk_at(fu_ref, off + r * count + i, wide), ml, mr, isl, half).astype(F32)
            for i in range(count)
        ]
        level += 1
    base_level = level
    top = [vals[0]]

    def ask(t):
        nb[2 * t] = top[0].astype(BF)
        mail.push(nb.at[2 * t], nb.at[2 * t + 1], nb_sem.at[t], {"row": r + (1 << t) * (1 - 2 * lax.rem(r >> t, 2))})

    def answer(t):
        mail.landed(nb.at[2 * t + 1], nb_sem.at[t], near_row)
        lev = base_level + t
        sib_ref[lev] = nb[2 * t + 1]
        if dev_count >> (lev + 1) > 1:
            other = nb[2 * t + 1].astype(F32)
            even = lax.rem(r >> t, 2) == 0
            lo = jnp.where(even, top[0], other)
            hi = jnp.where(even, other, top[0])
            at = dev_count - (dev_count >> lev) + ((me >> lev) >> 1)
            top[0] = combine(lo, hi, chunk_at(fv_ref, at, wide), chunk_at(fu_ref, at, wide), ml, mr, isl, half).astype(F32)
            ask(t + 1)

    row_levels = rows.bit_length() - 1
    ask(0)

    def relay_across():
        for e in range(1, inner):
            o = zi * inner + turn_x(e)
            mail.landed(xpart(o, 0), x_sem.at[o, 0], near_row)
            mail.push(xpart(o, 0), xpart(o, 0), x_sem.at[o, 0], row_of(zi + 1, xi), up)
            mail.push(xpart(o, 0), xpart(o, 0), x_sem.at[o, 0], row_of(zi - 1, xi), down)

    def relay_along(d, e, part):
        for back in (True, False):
            have = zi >= d if back else zi + d < deep
            oz = zi - d if back else zi + d
            o = oz * inner + turn_x(e)
            guarded(have, lambda o=o: mail.landed(xpart(o, part), x_sem.at[o, part], near_row))
            if d < deep - 1:
                onward = jnp.logical_and(have, up if back else down)
                mail.push(xpart(o, part), xpart(o, part), x_sem.at[o, part], row_of(zi + 1 if back else zi - 1, xi), onward)
            if part == 1:
                for f in range(1, inner):
                    mail.push(xpart(o, 1), xpart(o, 1), x_sem.at[o, 1], row_of(zi, turn_x(f)), have)

    def relay_points():
        if inner == 2:
            got = 2 * (1 - xi)
            mail.landed(xp.at[got], p_sem.at[got], near_row)
            to = lax.rem(zi + deep + 1 - 2 * xi, deep)
            mail.push(xp.at[got], xp.at[2 * xi], p_sem.at[2 * xi], row_of(to, xi))

    def relay_w(kind):
        for e in range(1, outer):
            o = lax.rem(oi + e, outer) * 2 + ki
            mail.landed(wa.at[o, kind], w_sem.at[o, kind], near_col)
            mail.push(wa.at[o, kind], wa.at[o, kind], w_sem.at[o, kind], {"col": oi * 2 + 1 - ki})

    def fill_w(kind, table):
        for e in range(outer):
            o = lax.rem(oi + e, outer) * 2 + 1 - ki
            mail.landed(wa.at[o, kind], w_sem.at[o, kind], near_col)
        for e in range(1, cols):
            o = lax.rem(c + e, cols)
            each_pack(lambda m, o=o: widen(wa[o, kind, m], table, 2 * (o * packs + m)))

    def fill_p():
        if inner == 2:
            mail.landed(xp.at[2 * xi], p_sem.at[2 * xi], near_row)
        else:
            mail.landed(xp.at[0], p_sem.at[0], near_row)
            mail.landed(xp.at[2], p_sem.at[2], near_row)
        for k in (0, 2):
            each_pack(lambda m, k=k: split(xp[k, m], ql, qr, 2 * (k * packs + m)))

    def products(pairs, mat, near, side, tables, out, piece, pieces):
        total = out.shape[0] // unroll
        def step(g, carry):
            for k in range(unroll):
                p = g * unroll + k
                i0, i1, j0, j1 = place(pairs, p)
                blk = mat[:, pl.ds(pl.multiple_of(p * wide, wide), wide)]
                if side == "z":
                    if not near:
                        reach = jnp.where(2 * p + 1 < live, wide, jnp.where(2 * p < live, half, 0))
                        blk = jnp.where(lane < reach, blk, none)
                    pair = jnp.concatenate([jnp.where(isl, blk, none), jnp.where(isl, none, blk)], axis=0)
                    out[p] = mm(jnp.where(isl, tables[i0], tables[i1]), pair)
                else:
                    out[p] = mm(blk, jnp.concatenate([tables[0][j0], tables[1][j1]], axis=0))
            return carry
        lax.fori_loop(piece * total // pieces, (piece + 1) * total // pieces, step, 0)

    def near_z(k, n):
        products((ni_ref, nj_ref), d_ref, True, "z", wp, pzn, k, n)

    def far_z(k, n):
        products((fi_ref, fj_ref), s_ref, False, "z", wc, pzc, k, n)

    def near_y(k, n):
        products((ni_ref, nj_ref), d_ref, True, "y", (ql, qr), pyn, k, n)

    def fill_rows(e):
        def step(dz, carry):
            o = lax.rem(zi + dz, deep) * inner + turn_x(e)
            for m in range(packs):
                split(xc[o, m], xl, xr, 2 * (o * packs + m))
            return carry
        lax.fori_loop(1 if e == 0 else 0, deep, step, 0)

    relay_across()
    relay_along(1, 0, 1)
    relay_along(1, 0, 0)
    for e in range(1, inner):
        relay_along(1, e, 0)
    relay_w(1)
    answer(0)
    if deep <= 2:
        relay_points()
        relay_w(0)
    for d in range(2, deep):
        relay_along(d, 0, 1)
        relay_along(d, 0, 0)
        if d == 2:
            relay_points()
            relay_w(0)
        for e in range(1, inner):
            relay_along(d, e, 0)
        if d == 2:
            if row_levels > 1:
                answer(1)
            fill_w(1, wp)
            near_z(0, 1)
            fill_w(0, wc)
            far_z(0, 2)
    if deep <= 2:
        fill_w(1, wp)
        near_z(0, 1)
        fill_w(0, wc)
        far_z(0, 2)
    far_z(1, 2)
    fill_rows(0)
    fill_p()
    near_y(0, 1)
    for t in range(2 if deep > 2 else 1, row_levels):
        answer(t)
    for e in range(1, inner):
        for dz in range(deep):
            o = lax.rem(zi + dz, deep) * inner + turn_x(e)
            mail.landed(xpart(o, 1), x_sem.at[o, 1], near_row)
        fill_rows(e)
    mail.close()


def pick(vals, at):
    out = vals[0]
    for i in range(1, len(vals)):
        out = jnp.where(at == i, vals[i], out)
    return out


def grant(own, operands):
    mib = 1024 * 1024
    return own // mib + 5 if own + operands < 40 * mib else min(62, (own + operands) // mib + 6)


def slot_kernel(rows, cols, unroll, fi_ref, fj_ref, ni_ref, nj_ref, live_ref, xl, xr, pyn, pzn, pzc, s_ref, y_ref, z_ref, n_ref,
                yc, yn, zc, zn, y0, y1):
    _, q, wide = xl.shape
    half = wide // 2
    packs = z_ref.shape[1]
    leaves = 2 * packs
    live = live_ref[0]
    isl = lax.broadcasted_iota(jnp.int32, (q, wide), 1) < half
    lane = lax.broadcasted_iota(jnp.int32, (q, wide), 1)
    none = jnp.zeros((q, wide), BF)
    blank = jnp.zeros((q, wide), F32)

    def clear(acc):
        group = 8
        def step(i, carry):
            for k in range(group):
                acc[i * group + k] = blank
            return carry
        lax.fori_loop(0, acc.shape[0] // group, step, 0)

    for acc in (yc, yn, zc, zn):
        clear(acc)

    def settle(pairs, p, yv, zv, ya, za):
        i0, i1, j0, j1 = place(pairs, p)
        a = ya[i0, :, :half] + yv[:, :half]
        b = ya[i1, :, half:] + yv[:, half:]
        c = za[j0, :, :half] + zv[:, :half]
        d = za[j1, :, half:] + zv[:, half:]
        ya[i0, :, :half] = a
        ya[i1, :, half:] = b
        za[j0, :, :half] = c
        za[j1, :, half:] = d

    def near_step(g, carry):
        for k in range(unroll):
            p = g * unroll + k
            settle((ni_ref, nj_ref), p, pyn[p], pzn[p], yn, zn)
        return carry

    lax.fori_loop(0, ni_ref.shape[1] // (2 * unroll), near_step, 0)

    def far(g, buf):
        for k in range(unroll):
            p = g * unroll + k
            settle((fi_ref, fj_ref), p, buf[k], pzc[p], yc, zc)

    def multiply(g, buf):
        for k in range(unroll):
            p = g * unroll + k
            j0, j1 = fj_ref[0, 2 * p], fj_ref[0, 2 * p + 1]
            blk = s_ref[:, pl.ds(pl.multiple_of(p * wide, wide), wide)]
            reach = jnp.where(2 * p + 1 < live, wide, jnp.where(2 * p < live, half, 0))
            blk = jnp.where(lane < reach, blk, none)
            top = xl[j0]
            bot = xr[j1]
            pair = jnp.concatenate([top, bot], axis=0)
            buf[k] = mm(blk, pair)

    steps = quot(live + 4 * unroll - 1, 4 * unroll)
    multiply(0, y0)
    def step(g, carry):
        multiply(2 * g + 1, y1)
        far(2 * g, y0)
        multiply(2 * g + 2, y0)
        far(2 * g + 1, y1)
        return carry
    lax.fori_loop(0, steps - 1, step, 0)
    multiply(2 * steps - 1, y1)
    far(2 * steps - 2, y0)
    far(2 * steps - 1, y1)

    def fold(acc, at):
        a, b = acc[at], acc[at + 1]
        return (jnp.where(isl, a, b) + pltpu.roll(jnp.where(isl, b, a), half, 1)).astype(BF)

    def out_y(i, carry):
        for m in range(packs):
            y_ref[i, 0, m] = fold(yc, 2 * (i * packs + m))
        return carry

    def out_p(i, carry):
        for m in range(packs):
            y_ref[i, 1, m] = fold(yn, 2 * (i * packs + m))
        return carry

    def out_z(i, carry):
        for m in range(packs):
            z_ref[i, m] = fold(zc, 2 * (i * packs + m))
        return carry

    def out_n(i, carry):
        for m in range(packs):
            n_ref[i, m] = fold(zn, 2 * (i * packs + m))
        return carry

    lax.fori_loop(0, cols, out_y, 0)
    lax.fori_loop(0, cols, out_p, 0)
    lax.fori_loop(0, rows, out_z, 0)
    lax.fori_loop(0, 3, out_n, 0)


def down_kernel(rows, cols, y_ref, z_ref, n_ref, sib_ref, order_ref, u_ref, v_ref, eu_ref, ev_ref, fu_ref, fv_ref,
                s_ref, o_ref, y_in, z1_in, z1_out, z2_in, zn_in, zn_out, ahead_y, ahead_z, u_turn, hot_turn,
                y_sem, z1_sem, z2_sem, n_sem):
    _, packs, q, wide = z_ref.shape
    half = wide // 2
    deep, inner = grid_of(rows)
    dev_count = rows * cols
    r = lax.axis_index("row")
    c = lax.axis_index("col")
    me = r * cols + c
    zi = r // inner
    xi = lax.rem(r, inner)
    bar = greet(rows, cols, r, c)
    ml, mr = left_mask(half, BF)
    isl = lax.broadcasted_iota(jnp.int32, (q, wide), 1) < half
    eye = twin_eye(half)
    pl.semaphore_wait(bar, rows + cols - 2)
    folded = inner == 2
    if folded:
        to = lax.rem(zi + deep - 1 + 2 * xi, deep) * inner + xi
        near = [push(n_ref.at[2 * xi], zn_in.at[0], n_sem, (0,), "row", to)]
    else:
        near = [
            push(n_ref.at[0], zn_in.at[0], n_sem, (0,), "row", lax.rem(r + rows - 1, rows)),
            push(n_ref.at[2], zn_in.at[1], n_sem, (1,), "row", lax.rem(r + 1, rows)),
        ]
    first = {}
    for d in list(range(1, deep)) + [0]:
        to = lax.rem(zi + d, deep) * inner
        first[d] = []
        for e in range(1, inner):
            peer = lax.rem(xi + e, inner)
            first[d].append(
                push(z_ref.at[to + peer], z1_in.at[d, e - 1], z1_sem, (d, e - 1), "row", zi * inner + peer)
            )
    y_copies = []
    for d in range(1, cols):
        peer = lax.rem(c + d, cols)
        y_copies.append(push(y_ref.at[peer], y_in.at[d - 1], y_sem, (d - 1,), "col", peer))

    levels = dev_count.bit_length() - 1
    lane_half = (lax.broadcasted_iota(jnp.int32, (q, wide), 1) >= half).astype(jnp.int32)

    def turned(v, chunk, side):
        return mm2(jnp.where(lane_half == side, v, 0.0), jnp.concatenate([chunk, chunk], axis=0), NT)

    y_down = z_down = None
    for level in range(levels - 1, -1, -1):
        own = me >> level
        side = lax.rem(own, 2)
        sib = sib_ref[level].astype(F32)
        rolled = pltpu.roll(sib, half, 1)
        xs = jnp.where(isl, sib, rolled)
        ws = jnp.where(isl, rolled, 0.0).astype(BF)
        at = dev_count - (dev_count >> level) + own // 2
        cup = chunk_at(s_ref, at, wide)
        dup = jnp.concatenate([cup, cup], axis=0)
        y_term = mm(jnp.where(lane_half == side, xs, 0.0).astype(BF), dup, NT)
        z_raw = jnp.where(lane_half == 1 - side, mm(ws, dup), 0.0)
        z_term = z_raw + pltpu.roll(z_raw, half, 1)
        if level < levels - 1:
            y_term = y_term + turned(y_down, chunk_at(fu_ref, at, wide), side)
            z_term = z_term + turned(z_down, chunk_at(fv_ref, at, wide), side)
        y_down, z_down = y_term, z_term

    second = []

    def pass_on(d):
        for copy in first[d]:
            copy.wait_recv()
        to = lax.rem(zi + d, deep) * inner + xi
        for m in range(packs):
            total = z_ref[to, m].astype(F32)
            for e in range(inner - 1):
                total = total + z1_in[d, e, m].astype(F32)
            z1_out[d - 1, m] = total.astype(BF)
        second.append(push(z1_out.at[d - 1], z2_in.at[d - 1], z2_sem, (d - 1,), "row", to))

    def pass_near():
        if folded:
            near[0].wait_recv()
            for m in range(packs):
                zn_out[m] = (zn_in[0, m].astype(F32) + n_ref[2 * (1 - xi), m].astype(F32)).astype(BF)
            near.append(push(zn_out, zn_in.at[1], n_sem, (1,), "row", zi * inner + 1 - xi))

    def columns(m):
        return slice(m * wide, (m + 1) * wide)

    if deep > 1:
        pass_on(1)
    pass_near()
    hi, lo = split2(y_down)
    hi, lo = diag2(hi, ml, mr), diag2(lo, ml, mr)
    for m in range(packs):
        e = eu_ref[:, columns(m)]
        ahead_y[m] = mm(e, hi, NT) + mm(e, lo, NT)
        ahead_z[m] = mm2(z_down, diag2(ev_ref[:, columns(m)], ml, mr), NT)
        u_turn[m] = mm(eye, diag2(u_ref[:, columns(m)], ml, mr), NT).astype(BF)
    if deep > 2:
        pass_on(2)
    hot_turn[...] = jnp.transpose(one_hot(order_ref, me * order_ref.shape[1]))
    for d in range(3, deep):
        pass_on(d)

    for copy in y_copies:
        copy.wait_recv()
    parts = []
    for m in range(packs):
        coef, raw = y_ref[c, 0, m].astype(F32), y_ref[c, 1, m].astype(F32)
        for d in range(cols - 1):
            coef = coef + y_in[d, 0, m].astype(F32)
            raw = raw + y_in[d, 1, m].astype(F32)
        leaf = (coef + ahead_y[m]).astype(BF)
        pts = (mm(u_turn[m], diag2(leaf, ml, mr)) + raw).astype(BF)
        parts.append(mm(eye, diag2(pts, ml, mr), NT).astype(BF))
    o_ref[:q] = mm(jnp.concatenate(parts, axis=1), hot_turn[...]).astype(BF)

    for copy in first[0] + second + near[1 if folded else 0:]:
        copy.wait_recv()
    parts = []
    for m in range(packs):
        coef, raw = z_ref[r, m].astype(F32), n_ref[1, m].astype(F32)
        for e in range(inner - 1):
            coef = coef + z1_in[0, e, m].astype(F32)
        for d in range(deep - 1):
            coef = coef + z2_in[d, m].astype(F32)
        for k in ((1,) if folded else (0, 1)):
            raw = raw + zn_in[k, m].astype(F32)
        leaf = (coef + ahead_z[m]).astype(BF)
        parts.append((mm(leaf, diag2(v_ref[:, columns(m)], ml, mr)) + raw).astype(BF))
    o_ref[q:] = mm(jnp.concatenate(parts, axis=1), hot_turn[...]).astype(BF)
    for copies in (*first.values(), second, near, y_copies):
        for copy in copies:
            copy.wait_send()


def per_device(
    x_vectors,
    w_vectors,
    order,
    ubasis,
    vbasis,
    leaf_up_u,
    leaf_up_v,
    coupling,
    coupling_pairs,
    coupling_count,
    near_blocks,
    near_pairs,
    transfer_u,
    transfer_v,
    upper_coupling,
):
    q, piece = x_vectors.shape
    rank = ubasis.shape[0]
    leaves = leaf_up_u.shape[1] // rank
    packs = leaves // 2
    wide = 2 * rank
    rows = lax.axis_size("row")
    cols = lax.axis_size("col")
    deep, inner = grid_of(rows)
    order2 = order.reshape(1, piece)

    def shape(*lead):
        return jax.ShapeDtypeStruct((*lead, q, wide), BF)

    def wide_shape(*lead):
        return jax.ShapeDtypeStruct((*lead, q, wide), F32)

    def buf(*lead, dtype=BF):
        return pltpu.VMEM((*lead, q, wide), dtype)

    def sems(*lead):
        return pltpu.SemaphoreType.DMA((2, *lead))

    def params(mib, cid=None):
        limit = mib * 1024 * 1024
        if cid is None:
            return pltpu.CompilerParams(vmem_limit_bytes=limit)
        return pltpu.CompilerParams(vmem_limit_bytes=limit, collective_id=cid, has_side_effects=True)

    token = pl.pallas_call(
        first_kernel,
        out_shape=jax.ShapeDtypeStruct((1, wide), F32),
        out_specs=VMEM,
        compiler_params=params(1),
        cost_estimate=pl.CostEstimate(flops=2_000_000_000, bytes_accessed=6_000_000, transcendentals=0),
    )()
    loaded = (token, coupling_pairs, near_pairs, order2, x_vectors, w_vectors, vbasis, ubasis, leaf_up_v, leaf_up_u)
    own_x, own_p, own_w, own_n, *spots = pl.pallas_call(
        local_kernel,
        out_shape=(
            shape(packs), shape(packs), shape(2, packs), shape(),
            *(jax.ShapeDtypeStruct((1, v.shape[1]), jnp.int32) for v in (coupling_pairs, coupling_pairs, near_pairs, near_pairs)),
        ),
        in_specs=[VMEM] * 10,
        out_specs=(VMEM,) * 8,
        compiler_params=params(12),
        cost_estimate=pl.CostEstimate(flops=8_000_000, bytes_accessed=20_000, transcendentals=0),
    )(*loaded)
    unroll = UNROLL
    far_pairs = coupling_pairs.shape[1] // 2
    near_pairs_count = near_pairs.shape[1] // 2
    levels = (rows * cols).bit_length() - 1
    row_levels = rows.bit_length() - 1
    tables = 2 * leaves * (3 + cols)
    raw = packs * (rows + 3 + 2 * cols)
    block = q * wide * 2
    x_left, x_right, p_y, p_z, c_z, sibs = pl.pallas_call(
        functools.partial(gather_kernel, rows, cols, 32),
        out_shape=(
            shape(rows * leaves), shape(rows * leaves), wide_shape(near_pairs_count), wide_shape(near_pairs_count),
            wide_shape(far_pairs), shape(levels),
        ),
        in_specs=[SMEM] * 5 + [VMEM] * 8,
        out_specs=(VMEM,) * 6,
        scratch_shapes=[
            buf(rows, packs),
            buf(3, packs),
            buf(cols, 2, packs),
            buf(cols),
            buf(2 * row_levels),
            buf(3 * leaves),
            buf(3 * leaves),
            buf(cols * leaves),
            buf(cols * leaves),
            pltpu.SemaphoreType.DMA((128,)),
            pltpu.SemaphoreType.DMA((rows, 2)),
            pltpu.SemaphoreType.DMA((3,)),
            pltpu.SemaphoreType.DMA((cols, 2)),
            pltpu.SemaphoreType.DMA((cols,)),
            pltpu.SemaphoreType.DMA((row_levels,)),
        ],
        compiler_params=params(6 + (tables + raw) * block // 1024**2, 0),
        cost_estimate=pl.CostEstimate(flops=20_000_000_000, bytes_accessed=60_000_000, transcendentals=0),
    )(
        *spots, coupling_count, own_x, own_p, own_w, own_n, transfer_u, transfer_v,
        coupling, near_blocks,
    )
    sums = leaves * (2 * cols + rows + 3) + 2 * unroll
    y_part, z_part, n_part = pl.pallas_call(
        functools.partial(slot_kernel, rows, cols, unroll),
        out_shape=(shape(cols, 2, packs), shape(rows, packs), shape(3, packs)),
        in_specs=[SMEM] * 5 + [VMEM] * 6,
        out_specs=(VMEM,) * 3,
        scratch_shapes=[
            buf(cols * leaves, dtype=F32),
            buf(cols * leaves, dtype=F32),
            buf(rows * leaves, dtype=F32),
            buf(3 * leaves, dtype=F32),
            buf(unroll, dtype=F32),
            buf(unroll, dtype=F32),
        ],
        compiler_params=params(grant(sums * 2 * block, 2 * rows * leaves * block + (near_pairs_count * 2 + far_pairs) * 2 * block + far_pairs * wide * q * 2)),
        cost_estimate=pl.CostEstimate(flops=20_000_000_000, bytes_accessed=60_000_000, transcendentals=0),
    )(*spots, coupling_count, x_left, x_right, p_y, p_z, c_z, coupling)
    out = pl.pallas_call(
        functools.partial(down_kernel, rows, cols),
        out_shape=jax.ShapeDtypeStruct((2 * q, piece), BF),
        in_specs=[VMEM] * 12,
        out_specs=VMEM,
        scratch_shapes=[
            buf(cols - 1, 2, packs),
            buf(deep, inner - 1, packs),
            buf(deep - 1, packs),
            buf(deep - 1, packs),
            buf(2, packs),
            buf(packs),
            buf(packs, dtype=F32),
            buf(packs, dtype=F32),
            buf(packs),
            pltpu.VMEM((piece, piece), BF),
            sems(cols - 1),
            sems(deep, inner - 1),
            sems(deep - 1),
            sems(2),
        ],
        compiler_params=params(20, 1),
    )(
        y_part, z_part, n_part, sibs, order2, ubasis, vbasis, leaf_up_u, leaf_up_v,
        transfer_u, transfer_v, upper_coupling,
    )
    return out[:q], out[q:]


def solution(mesh):
    both = P(None, ("row", "col"))
    flat = P(("row", "col"))
    return jax.shard_map(
        per_device,
        mesh=mesh,
        in_specs=(both, both, flat, both, both, both, both, both, both, flat, both, both, P(), P(), P()),
        out_specs=(both, both),
        check_vma=False,
    )
```
